32 devices in a mesh: ctx: 8 (over z, x), ch: 4 (over y, core).
Axes of the slice: x: 2, y: 2, z: 4, core: 2. Of those that a mesh axis runs over, the one named last changes fastest.
Arguments:
- query_input: bfloat16 [4096, 4096], P('ch', 'ctx'), may hold values from -6 to 6
- key_input: bfloat16 [4096, 4096], P('ch', 'ctx'), may hold values from -6 to 6
- value_input: bfloat16 [4096, 4096], P('ch', 'ctx'), may hold values from -6 to 6
- decay_rate: float32 [8, 16], P('ch'), may hold values from 0 to 1, as said below
- residue: float32 [8, 16], P('ch'), may hold values from -1 to 1
- doc_ends: int32 [4], replicated, may hold values from 1 to 4096, as said below
- out_weight: bfloat16 [4096, 4096], P(None, 'ch'), may hold values from -0.09375 to 0.09375
- out_cotangent: bfloat16 [4096, 4096], P('ctx', 'ch'), may hold values from -6 to 6
Outputs:
- query_grad: bfloat16 [4096, 4096], P('ch', 'ctx')
- key_grad: bfloat16 [4096, 4096], P('ch', 'ctx')
- value_grad: bfloat16 [4096, 4096], P('ch', 'ctx')
- weight_grad: float32 [4096, 4096], P('ctx', 'ch')
The draws below stay inside these ranges and needn't reach their ends.
Inputs may be any that keep to these rules, and one draw needn't show every extreme that they name: `doc_ends`: strictly increasing; the last entry equals 4096. `decay_rate`: positive.
All inputs are finite; a program needn't handle non-finite values.
Results may differ from the reference program's by a relative error of at most 0.0029.
Values may be sent and summed in bfloat16 or wider, within the bound.
A program may use at most 128 MiB of HBM per device.

```python
import math
from functools import partial
import jax
import jax.numpy as jnp
from jax import lax

D = 4096
GROUP_CH = 512
POLES = 16
TOK_DEV = 512
DOCS = 4
FILTERS = 8
CHANNELS = 4096
SEQ = 4096
N_CTX = 8


def filter_poles(key):
    base = jax.random.fold_in(key, 11)
    pick_key, slow_key, fast_key, sign_key = jax.random.split(base, 4)
    pole_shape = (FILTERS, POLES)
    slow_share = 0.5
    slow_pick = jax.random.uniform(pick_key, pole_shape, jnp.float32) < slow_share
    slow_decays = math.log(10.0) / SEQ * jnp.exp(jax.random.uniform(slow_key, pole_shape, jnp.float32, math.log(0.05), 0.0))
    fast_decays = jax.random.uniform(fast_key, pole_shape, jnp.float32, 1.0 / 50.0, 1.0 / 30.0)
    decays = jnp.where(slow_pick, slow_decays, fast_decays)
    amplitudes = jnp.clip(jax.random.normal(sign_key, pole_shape, jnp.float32), -4.0, 4.0) * jnp.sqrt(2.0 * decays) * 0.5
    return (decays, amplitudes)


def draw_decay_rate(key, part):
    return filter_poles(key)[0].astype(jnp.float32)


def draw_residue(key, part):
    return filter_poles(key)[1].astype(jnp.float32)


def draw_doc_ends(key, part):
    picks = jax.random.permutation(jax.random.fold_in(key, 23), SEQ - 1)[:DOCS - 1] + 1
    inner = jnp.sort(picks.astype(jnp.int32))
    return jnp.concatenate([inner, jnp.full((1,), SEQ, jnp.int32)]).astype(jnp.int32)


def shard_levels(stream_key, extent, shards, smallest, largest):
    def one(dim, shards_of):
        heights = jax.random.uniform(jax.random.fold_in(jax.random.fold_in(stream_key, 6), dim), (shards_of,), jnp.float32, smallest / len(shards), largest / len(shards))
        return jnp.repeat(jnp.exp(heights), extent[dim] // shards_of).reshape((-1,) + (1,) * (len(extent) - dim - 1))

    factor_of = one(*shards[0])
    for cut in shards[1:]:
        factor_of = factor_of * one(*cut)
    return factor_of


def centred(stream_key, extent, deviation, bound, cuts=(), kind=jnp.bfloat16):
    values = jax.random.normal(stream_key, extent, jnp.float32) * deviation
    if len(cuts) > 0:
        values = shard_levels(stream_key, extent, cuts, -0.22, 0.18) * values
    return jnp.clip(values, min=-bound, max=bound).astype(kind)


def setup_inputs(seed: int = 0) -> dict:
    keys = jax.random.split(jax.random.key(seed), 9)
    return {
        "query_input": centred(keys[0], (CHANNELS, SEQ), 1.0, 6.0, ((0, 4), (1, 8))),
        "key_input": centred(keys[1], (CHANNELS, SEQ), 1.0, 6.0, ((0, 4), (1, 8))),
        "value_input": centred(keys[2], (CHANNELS, SEQ), 1.0, 6.0, ((0, 4), (1, 8))),
        "decay_rate": draw_decay_rate(jax.random.fold_in(keys[8], 71), 0),
        "residue": draw_residue(jax.random.fold_in(keys[8], 71), 0),
        "doc_ends": draw_doc_ends(jax.random.fold_in(keys[8], 71), 0),
        "out_weight": centred(keys[6], (CHANNELS, D), CHANNELS ** -0.5, 0.09375, ((1, 4),)),
        "out_cotangent": centred(keys[7], (SEQ, D), 1.0, 6.0, ((0, 8), (1, 4))),
    }


def block_maps(block_index, doc_ids, decays, weights):
    anchor = (block_index * TOK_DEV).astype(jnp.int32)
    offsets = jnp.arange(TOK_DEV, dtype=jnp.int32)
    ids = lax.dynamic_slice_in_dim(doc_ids, anchor, TOK_DEV)
    previous = jnp.where(block_index > 0, doc_ids[jnp.maximum(anchor - 1, 0).astype(jnp.int32)], -1)
    place = offsets.astype(jnp.float32)
    lags = place[:, None] - place[None, :]
    causal = (lags >= 0.0) & (ids[:, None] == ids[None, :])
    powers = jnp.exp(-decays[:, None, None] * jnp.maximum(lags, 0.0)[None, :, :])
    kernel = jnp.einsum('n,nts->ts', weights, powers, precision=lax.Precision.HIGHEST)
    kernel = jnp.where(causal, kernel, 0.0)
    alive_mask = (ids == previous).astype(jnp.float32)
    tail_mask = (ids == ids[-1]).astype(jnp.float32)
    carry_in_map = weights[:, None] * jnp.exp(-decays[:, None] * (place + 1.0)[None, :]) * alive_mask[None, :]
    carry_out_map = jnp.exp(-decays[:, None] * (TOK_DEV - 1.0 - place)[None, :]) * tail_mask[None, :]
    back_out_map = jnp.exp(-decays[:, None] * place[None, :]) * alive_mask[None, :]
    back_in_map = weights[:, None] * jnp.exp(-decays[:, None] * (TOK_DEV - place)[None, :]) * tail_mask[None, :]
    transit = jnp.exp(-decays * TOK_DEV) * (ids[-1] == previous).astype(jnp.float32)
    return (kernel, carry_in_map, carry_out_map, back_out_map, back_in_map, transit)

def group_pass(doc_ids, operands):
    mixed, signal, decays, weights = operands
    group_ch = mixed.shape[0]
    mixed_blocks = mixed.reshape(group_ch, N_CTX, TOK_DEV).transpose(1, 0, 2)
    signal_blocks = signal.reshape(group_ch, N_CTX, TOK_DEV).transpose(1, 0, 2)
    block_ids = jnp.arange(N_CTX, dtype=jnp.int32)
    start_state = jnp.zeros((POLES, group_ch), jnp.float32)

    def forward_step(state, inputs):
        block_index, block_in = inputs
        kernel, carry_in_map, carry_out_map, back_out_map, back_in_map, transit = block_maps(block_index, doc_ids, decays, weights)
        result = jnp.dot(block_in, kernel.T, precision=lax.Precision.HIGHEST)
        result = result + jnp.dot(state.T, carry_in_map, precision=lax.Precision.HIGHEST)
        state = transit[:, None] * state + jnp.dot(carry_out_map, block_in.T, precision=lax.Precision.HIGHEST)
        return (state, result)

    def backward_step(state, inputs):
        block_index, block_grad = inputs
        kernel, carry_in_map, carry_out_map, back_out_map, back_in_map, transit = block_maps(block_index, doc_ids, decays, weights)
        result = jnp.dot(block_grad, kernel, precision=lax.Precision.HIGHEST)
        result = result + jnp.dot(state.T, back_in_map, precision=lax.Precision.HIGHEST)
        state = transit[:, None] * state + jnp.dot(back_out_map, block_grad.T, precision=lax.Precision.HIGHEST)
        return (state, result)
    final_fwd, filtered = lax.scan(forward_step, start_state, (block_ids, mixed_blocks))
    final_bwd, spread = lax.scan(backward_step, start_state, (block_ids, signal_blocks), reverse=True)
    filtered = filtered.transpose(1, 0, 2).reshape(group_ch, SEQ)
    spread = spread.transpose(1, 0, 2).reshape(group_ch, SEQ)
    return (filtered, spread)

def reference(query_input, key_input, value_input, decay_rate, residue, doc_ends, out_weight, out_cotangent):
    positions = jnp.arange(SEQ, dtype=jnp.int32)
    doc_ids = lax.optimization_barrier(jnp.sum((doc_ends[None, :] <= positions[:, None]).astype(jnp.int32), axis=1)).astype(jnp.int32)
    output_grad = jnp.dot(out_weight, out_cotangent.T, preferred_element_type=jnp.float32)
    query_f = query_input.astype(jnp.float32)
    key_f = key_input.astype(jnp.float32)
    value_f = value_input.astype(jnp.float32)
    mixed = key_f * value_f
    signal = output_grad * query_f
    mixed_groups = mixed.reshape(FILTERS, GROUP_CH, SEQ)
    signal_groups = signal.reshape(FILTERS, GROUP_CH, SEQ)
    filtered, spread = lax.map(partial(group_pass, doc_ids), (mixed_groups, signal_groups, decay_rate, residue))
    filtered = filtered.reshape(CHANNELS, SEQ)
    spread = spread.reshape(CHANNELS, SEQ)
    gated = (query_f * filtered).astype(jnp.bfloat16)
    query_grad = (output_grad * filtered).astype(jnp.bfloat16)
    key_grad = (spread * value_f).astype(jnp.bfloat16)
    value_grad = (spread * key_f).astype(jnp.bfloat16)
    weight_grad = jnp.dot(gated, out_cotangent, preferred_element_type=jnp.float32) * (1.0 / math.sqrt(SEQ))
    return (query_grad, key_grad, value_grad, weight_grad)
```

```python
import functools
import math

import jax
import jax.numpy as jnp
from jax import lax
from jax.experimental import pallas as pl
from jax.experimental.pallas import tpu as pltpu
from jax.sharding import PartitionSpec as P

MESH = pl.DeviceIdType.MESH
HIGH = lax.Precision.HIGH
TILE = 128
PARTS = 4
VMEM_LIMIT = 60 * 1024 * 1024


def doc_of(doc_ends, positions):
    return jnp.sum((doc_ends[None, :] <= positions[:, None]).astype(jnp.int32), axis=1)


def local_kernel(decay_rate, residue, doc_ids, length):
    groups = decay_rate.shape[0]
    place = jnp.arange(length, dtype=jnp.float32)
    narrow = jnp.arange(TILE, dtype=jnp.float32)
    half = 0.5 * TILE
    rising = jnp.exp(-decay_rate[:, None, :] * (place - half)[None, :, None]) * residue[:, None, :]
    falling = jnp.exp(decay_rate[:, None, :] * (narrow - half)[None, :, None])
    strip = jnp.einsum("gtn,gsn->gts", rising, falling, precision=lax.Precision.HIGHEST)
    columns = []
    for start in range(0, length, TILE):
        top = jnp.zeros((groups, start, TILE), jnp.float32)
        columns.append(jnp.concatenate([top, strip[:, : length - start]], axis=1))
    kernel = jnp.concatenate(columns, axis=2)
    offsets = jnp.arange(length, dtype=jnp.int32)
    causal = (offsets[:, None] >= offsets[None, :]) & (doc_ids[:, None] == doc_ids[None, :])
    return jnp.where(causal[None], kernel, 0.0)


def exchange_rows(gated, n_ctx, n_ch):
    rows, length = gated.shape
    mine = rows * n_ch // n_ctx
    pieces = gated.reshape(n_ctx // n_ch, n_ch, mine // n_ch, length)
    pieces = lax.all_to_all(pieces, "ch", split_axis=1, concat_axis=0, tiled=True)
    pieces = pieces.reshape(n_ctx, mine // n_ch, length)
    pieces = lax.all_to_all(pieces, "ctx", split_axis=0, concat_axis=0, tiled=True)
    pieces = pieces.transpose(1, 0, 2).reshape(mine // n_ch, n_ctx * length)
    return lax.all_gather(pieces, "ch", axis=0, tiled=True)


def ctx_id(index):
    return (index, lax.axis_index("ch"))


def ch_id(index):
    return (lax.axis_index("ctx"), index)


def remote(src, dst, send, recv, device):
    return pltpu.make_async_remote_copy(
        src_ref=src, dst_ref=dst, send_sem=send, recv_sem=recv, device_id=device, device_id_type=MESH
    )


def greet(devices):
    barrier = pltpu.get_barrier_semaphore()
    for device in devices:
        pl.semaphore_signal(barrier, inc=1, device_id=device, device_id_type=MESH)
    pl.semaphore_wait(barrier, len(devices))


def split(wide):
    high = wide.astype(jnp.bfloat16)
    return high, (wide - high.astype(jnp.float32)).astype(jnp.bfloat16)


def dot(a, b, dims):
    return lax.dot_general(a, b, (dims, ((), ())), preferred_element_type=jnp.float32)


def dot_split(a, b, dims):
    return dot(a[0], b[0], dims) + dot(a[0], b[1], dims) + dot(a[1], b[0], dims)


NN = ((1,), (0,))
NT = ((1,), (1,))


def stacked_left(states):
    high, low = split(states)
    high, low = high.astype(jnp.float32), low.astype(jnp.float32)
    return jnp.concatenate([high, low, high], axis=0).T.astype(jnp.bfloat16)


def stacked_right(maps):
    high, low = split(maps)
    return jnp.concatenate([high, high, low], axis=0)


def column(row):
    n = row.shape[1]
    same = lax.broadcasted_iota(jnp.int32, (n, n), 0) == lax.broadcasted_iota(jnp.int32, (n, n), 1)
    return jnp.sum(jnp.where(same, jnp.broadcast_to(row, (n, n)), 0.0), axis=1, keepdims=True)


def fused_kernel(
    docs_ref, decay_ref, residue_ref, query_hbm, key_hbm, value_hbm, weight_hbm, cot_hbm,
    query_grad_hbm, key_grad_hbm, value_grad_hbm, weight_grad_hbm,
    query, key, value, cots, weights, partial, arrived, across_out, across_in,
    kernel_high, kernel_low, mixed_high, mixed_low, filtered_ref, gated_ref, turned, rows_ref,
    grads, acc, half_out, half_in, part_ref, twin_part, slots, joint, back_part, back_twin, back_slots, back_joint,
    in_maps, back_maps,
    load_sem, weight_sem, store_sem, own_sem,
    z_send, z_recv, half_send, half_recv,
    far_send, far_recv, across_send, across_recv,
    s_send, s_recv, sz_send, sz_recv, b_send, b_recv, bz_send, bz_recv,
    turn_send, turn_recv, join_send, join_recv, wide_send, wide_recv,
):
    f32, bf16 = jnp.float32, jnp.bfloat16
    me, ch = lax.axis_index("ctx"), lax.axis_index("ch")
    z, x = me // 2, me % 2
    twin = me + 1 - 2 * x
    y, core = ch // 2, ch % 2
    across = (1 - y) * 2 + core
    mate = y * 2 + 1 - core
    far = (1 - y) * 2 + 1 - core
    length, width = cots.shape[1], cots.shape[2]
    rows_all = query.shape[0]
    half_rows = rows_all // 2
    piece = turned.shape[1]
    poles = part_ref.shape[1]
    part_width = width // PARTS

    greet(
        [ctx_id(twin)]
        + [ctx_id(lax.rem(me + 2 * d, 8)) for d in range(1, 4)]
        + [ch_id(lax.rem(ch + d, 4)) for d in range(1, 4)]
    )

    parts = [pl.ds(p * part_width, part_width) for p in range(PARTS)]

    def goes(side):
        return z < 3 if side > 0 else z > 0

    def along(origin, side, p, src=None):
        to = cots.at[origin, :, parts[p]]
        src = to if src is None else src.at[:, parts[p]]
        return remote(src, to, z_send.at[(side + 1) // 2, p, origin], z_recv.at[p, origin], ctx_id(me + 2 * side))

    def own_along(p):
        for side in (1, -1):

            @pl.when(goes(side))
            def _():
                along(z, side, p, cot_hbm).start()

    own_along(0)

    loads = [
        pltpu.make_async_copy(src, to, load_sem.at[k])
        for k, (src, to) in enumerate(((cot_hbm, cots.at[z]), (key_hbm, key), (value_hbm, value), (query_hbm, query)))
    ]
    weight_loads = [
        pltpu.make_async_copy(
            weight_hbm.at[pl.ds(pl.multiple_of(index * rows_all, rows_all), rows_all)], weights.at[k], weight_sem.at[k]
        )
        for k, index in enumerate((far, across, mate, ch))
    ]
    for copy in [loads[0], weight_loads[0]] + loads[1:3] + [weight_loads[1], loads[3]] + weight_loads[2:]:
        copy.start()
    own_along(1)

    def step(s, p):
        for side in (1, -1):
            origin = z - side * s

            @pl.when((origin >= 0) & (origin <= 3))
            def _():
                along(origin, side, p).wait_recv()

                @pl.when(goes(side))
                def _():
                    along(origin, side, p).start()

    def doc_at(position):
        total = jnp.int32(0)
        for k in range(docs_ref.shape[0]):
            total = total + jnp.where(docs_ref[k] <= position, 1, 0)
        return total

    start = me * length
    last = doc_at(start + length - 1)
    previous = jnp.where(me > 0, doc_at(start - 1), -1)

    def docs_of(offsets):
        total = jnp.zeros(offsets.shape, jnp.int32)
        for k in range(docs_ref.shape[0]):
            total = total + jnp.where(docs_ref[k] <= offsets + start, 1, 0)
        return total

    lanes = lax.broadcasted_iota(jnp.int32, (1, length), 1)
    ids_row = docs_of(lanes)
    ids_column = docs_of(lax.broadcasted_iota(jnp.int32, (length, 1), 0))
    alive = jnp.where(ids_row == previous, 1.0, 0.0)
    tail = jnp.where(ids_row == last, 1.0, 0.0)
    place = lanes.astype(f32)
    rates = [column(decay_ref[pl.ds(g, 1), :]) for g in range(2)]
    gains = [column(residue_ref[pl.ds(g, 1), :]) for g in range(2)]

    tile = TILE
    shift = 0.5 * tile
    near_place = lax.broadcasted_iota(jnp.int32, (1, tile), 1).astype(f32)
    causal_rows = lax.broadcasted_iota(jnp.int32, (length, tile), 0)
    causal_columns = lax.broadcasted_iota(jnp.int32, (length, tile), 1)
    out_maps, adjoint_maps = [], []
    for g in range(2):
        rate, gain = rates[g], gains[g]
        rising = gain * jnp.exp(-rate * (place - shift))
        falling = jnp.exp(rate * (near_place - shift))
        strip = dot(stacked_left(rising), stacked_right(falling), NN)
        for b in range(length // tile):
            s0 = b * tile
            columns = pl.ds(s0, tile)
            same = (causal_rows[: length - s0] >= causal_columns[: length - s0]) & (
                ids_column[s0:] == ids_row[:, s0 : s0 + tile]
            )
            high, low = split(jnp.where(same, strip[: length - s0], 0.0))
            kernel_high[g, pl.ds(s0, length - s0), columns] = high
            kernel_low[g, pl.ds(s0, length - s0), columns] = low
            if b > 0:
                kernel_high[g, pl.ds(0, s0), columns] = jnp.zeros((s0, tile), bf16)
                kernel_low[g, pl.ds(0, s0), columns] = jnp.zeros((s0, tile), bf16)
        out_maps.append(split(jnp.exp(-rate * (length - 1.0 - place)) * tail))
        adjoint_maps.append(split(jnp.exp(-rate * place) * alive))
        in_maps[g] = stacked_right(gain * jnp.exp(-rate * (place + 1.0)) * alive)
        back_maps[g] = stacked_right(gain * jnp.exp(-rate * (length - place)) * tail)

    def multiply(k, store):
        weight_loads[k].wait()

        @pl.loop(0, 4)
        def _(r):
            rows = pl.ds(pl.multiple_of(r * 2 * piece, piece), 2 * piece)
            store(rows, dot(weights[k, rows, :], cots[z], NT))

    def to_partial(k):
        def store(rows, product):
            partial[k, rows, :] = product

        return store

    to_mate = [
        remote(partial.at[k], arrived.at[k], far_send.at[k], far_recv.at[k], ch_id(mate)) for k in range(2)
    ]
    loads[0].wait()
    multiply(0, to_partial(0))
    to_mate[0].start()

    loads[1].wait()
    loads[2].wait()

    @pl.loop(0, 8)
    def _(r):
        rows = pl.ds(pl.multiple_of(r * piece, piece), piece)
        high, low = split(key[rows, :].astype(f32) * value[rows, :].astype(f32))
        mixed_high[rows, :] = high
        mixed_low[rows, :] = low

    def state_of(g, maps):
        rows = pl.ds(g * half_rows, half_rows)
        return dot_split(maps, (mixed_high[rows, :], mixed_low[rows, :]), NT)

    for g in range(2):
        part_ref[g] = state_of(g, out_maps[g])
    to_twin_state = remote(part_ref, twin_part, s_send, s_recv, ctx_id(twin))
    to_twin_state.start()

    chunks = [pl.ds(r * 2 * piece, 2 * piece) for r in range(4)]
    across_copies = [
        remote(across_out.at[rows], across_in.at[rows], across_send.at[r], across_recv.at[r], ch_id(across))
        for r, rows in enumerate(chunks)
    ]
    weight_loads[1].wait()
    to_mate[0].wait_recv()
    for r, rows in enumerate(chunks):
        total = dot(weights[1, rows, :], cots[z], NT) + arrived[0, rows, :]
        across_out[rows, :] = total.astype(bf16)
        across_copies[r].start()

    first_half = jnp.where(x == 0, 1.0, 0.0)
    second_half = 1.0 - first_half
    plane_first = doc_at((2 * z + 1) * length - 1)
    plane_last = doc_at((2 * z + 2) * length - 1)
    plane_before = jnp.where(z > 0, doc_at(2 * z * length - 1), -1)
    first_whole = jnp.where(plane_first == plane_before, 1.0, 0.0)
    second_whole = jnp.where(plane_first == plane_last, 1.0, 0.0)
    decays = [jnp.exp(-rates[g] * float(length)) for g in range(2)]
    whole_decays = [jnp.exp(-rates[g] * (2.0 * length)) * (first_whole * second_whole) for g in range(2)]

    to_twin_state.wait_recv()
    for g in range(2):
        through = decays[g] * second_whole
        joint[g] = part_ref[g] * (first_half * through + second_half) + twin_part[g] * (
            first_half + second_half * through
        )
    chain = remote(joint, slots, sz_send, sz_recv, ctx_id(me + 2))

    @pl.when(z == 0)
    def _():
        slots[...] = jnp.zeros_like(slots)
        chain.start()

    own_along(2)

    for g in range(2):

        @pl.loop(0, 2)
        def _(r):
            rows = pl.ds(pl.multiple_of(g * half_rows + r * 2 * piece, piece), 2 * piece)
            filtered_ref[rows, :] = dot_split(
                (mixed_high[rows, :], mixed_low[rows, :]), (kernel_high[g], kernel_low[g]), NT
            )

    multiply(2, to_partial(1))
    to_mate[1].start()
    own_along(3)
    multiply(3, to_partial(2))

    @pl.when(z > 0)
    def _():
        chain.wait_recv()

        @pl.when(z < 3)
        def _():
            for g in range(2):
                joint[g] += slots[g] * whole_decays[g]
            chain.start()

    step(1, 0)
    step(1, 1)
    loads[3].wait()

    for g in range(2):
        entering = slots[g] * (first_half + second_half * decays[g] * first_whole) + twin_part[g] * second_half
        carried = stacked_left(entering)
        for r in range(4):
            rows = pl.ds(g * half_rows + r * piece, piece)
            filtered = filtered_ref[rows, :] + dot(carried[r * piece : (r + 1) * piece], in_maps[g], NN)
            filtered_ref[rows, :] = filtered
            gated_ref[g, r] = (query[rows, :].astype(f32) * filtered).astype(bf16)

    turns = []
    for d in range(1, 4):
        to = lax.rem(ch + d, 4)
        came = lax.rem(ch + 4 - d, 4)
        for h in range(2):
            slot = 2 * d + h
            out = remote(gated_ref.at[h, to], turned.at[2 * ch + h], turn_send.at[slot], turn_recv.at[slot], ch_id(to))
            out.start()
            back = remote(
                gated_ref.at[h, to], turned.at[2 * came + h], turn_send.at[slot], turn_recv.at[slot], ch_id(to)
            )
            turns.append((out, back))
    own_turns = [pltpu.make_async_copy(gated_ref.at[h, ch], turned.at[2 * ch + h], own_sem.at[h]) for h in range(2)]
    for copy in own_turns:
        copy.start()
    step(1, 2)

    to_mate[1].wait_recv()
    for copy in across_copies:
        copy.wait_recv()

    @pl.loop(0, 8)
    def _(r):
        rows = pl.ds(pl.multiple_of(r * piece, piece), piece)
        output_grad = partial[2, rows, :] + arrived[1, rows, :] + across_in[rows, :].astype(f32)
        high, low = split(output_grad * query[rows, :].astype(f32))
        mixed_high[rows, :] = high
        mixed_low[rows, :] = low
        grads[0, rows, :] = (output_grad * filtered_ref[rows, :]).astype(bf16)

    for g in range(2):
        back_part[g] = state_of(g, adjoint_maps[g])
    back_twin_state = remote(back_part, back_twin, b_send, b_recv, ctx_id(twin))
    back_twin_state.start()
    stores = [
        pltpu.make_async_copy(grads.at[k], to, store_sem.at[k])
        for k, to in enumerate((query_grad_hbm, key_grad_hbm, value_grad_hbm))
    ]
    stores[0].start()
    for g in range(2):

        @pl.loop(0, 2)
        def _(r):
            rows = pl.ds(pl.multiple_of(g * half_rows + r * 2 * piece, piece), 2 * piece)
            filtered_ref[rows, :] = dot_split(
                (mixed_high[rows, :], mixed_low[rows, :]), (kernel_high[g], kernel_low[g]), NN
            )

    back_twin_state.wait_recv()
    for g in range(2):
        through = decays[g] * first_whole
        back_joint[g] = back_part[g] * (second_half * through + first_half) + back_twin[g] * (
            second_half + first_half * through
        )
    back_chain = remote(back_joint, back_slots, bz_send, bz_recv, ctx_id(me - 2))

    @pl.when(z == 3)
    def _():
        back_slots[...] = jnp.zeros_like(back_slots)
        back_chain.start()

    @pl.when(z < 3)
    def _():
        back_chain.wait_recv()

        @pl.when(z > 0)
        def _():
            for g in range(2):
                back_joint[g] += back_slots[g] * whole_decays[g]
            back_chain.start()

    for copy in own_turns:
        copy.wait()
    for out, back in turns:
        back.wait_recv()

    def rows_of(index):
        return pl.ds(pl.multiple_of(index * piece, piece), piece)

    def columns_of(plane):
        return pl.ds(pl.multiple_of(plane * length, 128), length)

    joins = []
    for d in range(1, 4):
        to = lax.rem(z + d, 4)
        out = remote(
            turned.at[pl.ds(2 * to, 2)],
            rows_ref.at[:, rows_of(ch), columns_of(z)],
            join_send.at[to],
            join_recv.at[z],
            ctx_id(2 * to + x),
        )
        out.start()
        joins.append(out)
    own_join = pltpu.make_async_copy(
        turned.at[pl.ds(2 * z, 2)], rows_ref.at[:, rows_of(ch), columns_of(z)], own_sem.at[2]
    )
    own_join.start()

    middle = (z * (3 - z)) // 2
    way = 1 - 2 * (z // 2)
    order = [z + way * (k - middle * c) for k, c in enumerate((0, 2, 1, 1))]

    def wide(slot, k, owner, to):
        block = rows_ref.at[:, rows_of(owner), columns_of(order[k])]
        return remote(block, block, wide_send.at[slot, k], wide_recv.at[slot, k], ch_id(to))

    def wide_start(k):
        if k == 0:
            own_join.wait()
        else:
            source = order[k]
            block = rows_ref.at[:, rows_of(ch), columns_of(source)]
            remote(block, block, join_send.at[source], join_recv.at[source], ctx_id(2 * source + x)).wait_recv()
        wide(0, k, ch, across).start()
        wide(1, k, ch, mate).start()

    def wide_on(k):
        wide(0, k, across, across).wait_recv()
        wide(2, k, across, mate).start()

    wide_start(0)
    step(1, 3)
    step(2, 0)

    for g in range(2):
        returning = back_slots[g] * (second_half + first_half * decays[g] * second_whole) + back_twin[g] * first_half
        carried = stacked_left(returning)
        for r in range(4):
            rows = pl.ds(g * half_rows + r * piece, piece)
            spread = filtered_ref[rows, :] + dot(carried[r * piece : (r + 1) * piece], back_maps[g], NN)
            grads[1, rows, :] = (spread * value[rows, :].astype(f32)).astype(bf16)
            grads[2, rows, :] = (spread * key[rows, :].astype(f32)).astype(bf16)
    stores[1].start()
    stores[2].start()

    step(2, 1)
    wide_start(1)
    wide_on(0)
    step(2, 2)
    wide_start(2)
    wide_on(1)
    wide_start(3)
    wide_on(2)
    step(2, 3)
    wide_on(3)

    norm_factor = 1.0 / math.sqrt(8 * length)

    def product(k, half, columns):
        return dot(rows_ref[half, :, columns_of(order[k])], cots[order[k], :, columns], NN)

    def add(k):
        wide(1, k, mate, mate).wait_recv()
        wide(2, k, far, mate).wait_recv()
        for half in range(2):

            @pl.loop(0, PARTS)
            def _(p):
                columns = pl.ds(pl.multiple_of(p * part_width, part_width), part_width)
                total = product(k, half, columns)
                acc[half, :, columns] = total if k == 0 else acc[half, :, columns] + total

    for k in range(3):
        add(k)
    wide(1, 3, mate, mate).wait_recv()
    wide(2, 3, far, mate).wait_recv()
    halves = [
        remote(half_out.at[:, parts[p]], half_in.at[:, parts[p]], half_send.at[p], half_recv.at[p], ctx_id(twin))
        for p in range(PARTS)
    ]
    store_acc = [
        pltpu.make_async_copy(acc.at[x, :, parts[p]], weight_grad_hbm.at[:, parts[p]], store_sem.at[3 + p])
        for p in range(PARTS)
    ]

    def finish(p):
        halves[p].wait_recv()
        acc[x, :, parts[p]] += half_in[:, parts[p]].astype(f32)
        store_acc[p].start()

    for p in range(PARTS):

        @pl.when(middle == 0)
        def _():
            along(order[3], 1, p).wait_recv()

        half_out[:, parts[p]] = ((acc[1 - x, :, parts[p]] + product(3, 1 - x, parts[p])) * norm_factor).astype(bf16)
        halves[p].start()
        acc[x, :, parts[p]] = (acc[x, :, parts[p]] + product(3, x, parts[p])) * norm_factor
        if p > 0:
            finish(p - 1)
    finish(PARTS - 1)

    for origin in range(4):
        for side in (1, -1):

            @pl.when(goes(side) & (origin <= z if side > 0 else origin >= z))
            def _():
                for p in range(PARTS):
                    along(origin, side, p).wait_send()

    @pl.when(z < 3)
    def _():
        chain.wait_send()

    @pl.when(z > 0)
    def _():
        back_chain.wait_send()

    for copy in to_mate + across_copies + [to_twin_state, back_twin_state] + joins + halves:
        copy.wait_send()
    for out, back in turns:
        out.wait_send()
    for k in range(4):
        wide(0, k, ch, across).wait_send()
        wide(1, k, ch, mate).wait_send()
        wide(2, k, across, mate).wait_send()
    for copy in stores + store_acc:
        copy.wait()


def fused(query_input, key_input, value_input, decay_rate, residue, doc_ends, out_weight, out_cotangent):
    rows, length = query_input.shape
    width = out_cotangent.shape[1]
    groups, poles = decay_rate.shape
    n_ctx, n_ch = lax.axis_size("ctx"), lax.axis_size("ch")
    piece = rows // 2 // n_ch
    anywhere = pl.BlockSpec(memory_space=pl.ANY)
    vmem = pl.BlockSpec(memory_space=pltpu.VMEM)
    smem = pl.BlockSpec(memory_space=pltpu.SMEM)
    f32, bf16 = jnp.float32, jnp.bfloat16
    dma = pltpu.SemaphoreType.DMA
    state = (groups, poles, rows // groups)
    maps = (groups, 3 * poles, length)
    block = (rows, length)
    return pl.pallas_call(
        fused_kernel,
        out_shape=tuple(jax.ShapeDtypeStruct(block, bf16) for _ in range(3))
        + (jax.ShapeDtypeStruct((rows // 2, width), f32),),
        in_specs=[smem, vmem, vmem] + [anywhere] * 5,
        out_specs=(anywhere,) * 4,
        scratch_shapes=[
            pltpu.VMEM(block, bf16), pltpu.VMEM(block, bf16), pltpu.VMEM(block, bf16),
            pltpu.VMEM((4, length, width), bf16),
            pltpu.VMEM((n_ch, rows, width), bf16),
            pltpu.VMEM((3,) + block, f32),
            pltpu.VMEM((2,) + block, f32),
            pltpu.VMEM(block, bf16), pltpu.VMEM(block, bf16),
            pltpu.VMEM((groups, length, length), bf16), pltpu.VMEM((groups, length, length), bf16),
            pltpu.VMEM(block, bf16), pltpu.VMEM(block, bf16),
            pltpu.VMEM(block, f32),
            pltpu.VMEM((2, n_ch, piece, length), bf16),
            pltpu.VMEM((n_ctx, piece, length), bf16),
            pltpu.VMEM((2, rows // 2, 4 * length), bf16),
            pltpu.VMEM((3,) + block, bf16),
            pltpu.VMEM((2, rows // 2, width), f32),
            pltpu.VMEM((rows // 2, width), bf16), pltpu.VMEM((rows // 2, width), bf16),
            pltpu.VMEM(state, f32), pltpu.VMEM(state, f32), pltpu.VMEM(state, f32), pltpu.VMEM(state, f32),
            pltpu.VMEM(state, f32), pltpu.VMEM(state, f32), pltpu.VMEM(state, f32), pltpu.VMEM(state, f32),
            pltpu.VMEM(maps, bf16), pltpu.VMEM(maps, bf16),
            dma((4,)), dma((4,)), dma((3 + PARTS,)), dma((3,)),
            dma((2, PARTS, 4)), dma((PARTS, 4)), dma((PARTS,)), dma((PARTS,)),
            dma((2,)), dma((2,)), dma((4,)), dma((4,)),
            dma(()), dma(()), dma(()), dma(()), dma(()), dma(()), dma(()), dma(()),
            dma((8,)), dma((8,)), dma((4,)), dma((4,)), dma((3, 4)), dma((3, 4)),
        ],
        compiler_params=pltpu.CompilerParams(
            collective_id=0, has_side_effects=True, vmem_limit_bytes=VMEM_LIMIT
        ),
        cost_estimate=pl.CostEstimate(flops=10_000_000_000, bytes_accessed=30_000_000, transcendentals=100_000),
        name="fused",
    )(doc_ends, decay_rate, residue, query_input, key_input, value_input, out_weight, out_cotangent)


def move_by_collectives(cotangent, weight, part, near, query, ahead, behind, in_map, out_map):
    n_ctx, n_ch = lax.axis_size("ctx"), lax.axis_size("ch")
    groups = part.shape[0]
    rows, length = query.shape
    query_f = query.astype(jnp.float32)
    cots = lax.all_gather(cotangent, "ctx", axis=0, tiled=True)
    partial_grad = lax.dot_general(
        weight, cotangent, (((1,), (1,)), ((), ())), preferred_element_type=jnp.float32
    )
    output_grad = lax.psum_scatter(partial_grad, "ch", scatter_dimension=0, tiled=True)
    entering = jnp.sum(ahead * lax.all_gather(part, "ctx", axis=0), axis=0)
    carried = jnp.einsum("gnc,gnt->gct", entering, in_map, precision=HIGH).reshape(rows, length)
    filtered = near + carried
    gathered = exchange_rows((query_f * filtered).astype(jnp.bfloat16), n_ctx, n_ch)
    signal = output_grad * query_f
    back_part = jnp.einsum("gnl,gcl->gnc", out_map, signal.reshape(groups, rows // groups, length), precision=HIGH)
    returning = jnp.sum(behind * lax.all_gather(back_part, "ctx", axis=0), axis=0)
    query_grad = (output_grad * filtered).astype(jnp.bfloat16)
    return signal, query_grad, returning, gathered, cots


def local(
    query_input, key_input, value_input, decay_rate, residue, doc_ends, out_weight, out_cotangent
):
    rows_here, length = query_input.shape
    n_ctx, n_ch = lax.axis_size("ctx"), lax.axis_size("ch")
    groups = decay_rate.shape[0]
    if (n_ctx, n_ch, groups) == (8, 4, 2) and rows_here == 1024 and length == 512:
        return fused(
            query_input, key_input, value_input, decay_rate, residue, doc_ends, out_weight, out_cotangent
        )
    group_rows = rows_here // groups
    me = lax.axis_index("ctx")
    offsets = jnp.arange(length, dtype=jnp.int32)
    place = offsets.astype(jnp.float32)
    doc_ids = doc_of(doc_ends, me * length + offsets)
    blocks = jnp.arange(n_ctx, dtype=jnp.int32)
    last_ids = doc_of(doc_ends, (blocks + 1) * length - 1)
    previous = jnp.where(me > 0, jnp.sum((doc_ends <= me * length - 1).astype(jnp.int32)), -1)
    last = doc_ids[-1]

    alive_mask = (doc_ids == previous).astype(jnp.float32)
    tail_mask = (doc_ids == last).astype(jnp.float32)
    rate = decay_rate[:, :, None]
    carry_in_map = residue[:, :, None] * jnp.exp(-rate * (place + 1.0)) * alive_mask
    carry_out_map = jnp.exp(-rate * (length - 1.0 - place)) * tail_mask
    back_out_map = jnp.exp(-rate * place) * alive_mask
    back_in_map = residue[:, :, None] * jnp.exp(-rate * (length - place)) * tail_mask
    steps_ahead = me - 1 - blocks
    joined_ahead = (steps_ahead >= 0) & (last_ids == previous)
    ahead_weight = jnp.where(
        joined_ahead[:, None, None],
        jnp.exp(-decay_rate[None] * (length * jnp.maximum(steps_ahead, 0)).astype(jnp.float32)[:, None, None]),
        0.0,
    )
    steps_back = blocks - 1 - me
    before_ids = jnp.concatenate([jnp.full((1,), -1, jnp.int32), last_ids[:-1]])
    joined_back = (steps_back >= 0) & (before_ids == last)
    back_weight = jnp.where(
        joined_back[:, None, None],
        jnp.exp(-decay_rate[None] * (length * jnp.maximum(steps_back, 0)).astype(jnp.float32)[:, None, None]),
        0.0,
    )

    key_f = key_input.astype(jnp.float32)
    value_f = value_input.astype(jnp.float32)
    mixed = (key_f * value_f).reshape(groups, group_rows, length)
    forward_part = jnp.einsum("gnl,gcl->gnc", carry_out_map, mixed, precision=HIGH)
    kernel = local_kernel(decay_rate, residue, doc_ids, length)
    near = jnp.einsum("gcs,gts->gct", mixed, kernel, precision=HIGH).reshape(rows_here, length)
    wide = (n_ctx,) + forward_part.shape
    signal, query_grad, returning, gated_rows, cotangent_all = move_by_collectives(
        out_cotangent,
        out_weight,
        forward_part,
        near,
        query_input,
        jnp.broadcast_to(ahead_weight[..., None], wide),
        jnp.broadcast_to(back_weight[..., None], wide),
        carry_in_map,
        back_out_map,
    )
    signal = signal.reshape(groups, group_rows, length)
    spread = jnp.einsum("gct,gts->gcs", signal, kernel, precision=HIGH)
    spread = spread + jnp.einsum("gnc,gns->gcs", returning, back_in_map, precision=HIGH)
    spread = spread.reshape(rows_here, length)
    key_grad = (spread * value_f).astype(jnp.bfloat16)
    value_grad = (spread * key_f).astype(jnp.bfloat16)

    norm_factor = 1.0 / math.sqrt(length * n_ctx)
    weight_grad = jnp.dot(gated_rows, cotangent_all, preferred_element_type=jnp.float32) * norm_factor
    return (query_grad, key_grad, value_grad, weight_grad)


def solution(mesh):
    return jax.shard_map(
        local,
        mesh=mesh,
        in_specs=(
            P("ch", "ctx"),
            P("ch", "ctx"),
            P("ch", "ctx"),
            P("ch", None),
            P("ch", None),
            P(),
            P(None, "ch"),
            P("ctx", "ch"),
        ),
        out_specs=(P("ch", "ctx"), P("ch", "ctx"), P("ch", "ctx"), P("ctx", "ch")),
        check_vma=False,
    )
```

```python
import functools
import math

import jax
import jax.numpy as jnp
from jax import lax
from jax.experimental import pallas as pl
from jax.experimental.pallas import tpu as pltpu
from jax.sharding import PartitionSpec as P

MESH = pl.DeviceIdType.MESH
HIGH = lax.Precision.HIGH
TILE = 128
PARTS = 4
VMEM_LIMIT = 60 * 1024 * 1024


def doc_of(doc_ends, positions):
    return jnp.sum((doc_ends[None, :] <= positions[:, None]).astype(jnp.int32), axis=1)


def local_kernel(decay_rate, residue, doc_ids, length):
    groups = decay_rate.shape[0]
    place = jnp.arange(length, dtype=jnp.float32)
    narrow = jnp.arange(TILE, dtype=jnp.float32)
    half = 0.5 * TILE
    rising = jnp.exp(-decay_rate[:, None, :] * (place - half)[None, :, None]) * residue[:, None, :]
    falling = jnp.exp(decay_rate[:, None, :] * (narrow - half)[None, :, None])
    strip = jnp.einsum("gtn,gsn->gts", rising, falling, precision=lax.Precision.HIGHEST)
    columns = []
    for start in range(0, length, TILE):
        top = jnp.zeros((groups, start, TILE), jnp.float32)
        columns.append(jnp.concatenate([top, strip[:, : length - start]], axis=1))
    kernel = jnp.concatenate(columns, axis=2)
    offsets = jnp.arange(length, dtype=jnp.int32)
    causal = (offsets[:, None] >= offsets[None, :]) & (doc_ids[:, None] == doc_ids[None, :])
    return jnp.where(causal[None], kernel, 0.0)


def exchange_rows(gated, n_ctx, n_ch):
    rows, length = gated.shape
    mine = rows * n_ch // n_ctx
    pieces = gated.reshape(n_ctx // n_ch, n_ch, mine // n_ch, length)
    pieces = lax.all_to_all(pieces, "ch", split_axis=1, concat_axis=0, tiled=True)
    pieces = pieces.reshape(n_ctx, mine // n_ch, length)
    pieces = lax.all_to_all(pieces, "ctx", split_axis=0, concat_axis=0, tiled=True)
    pieces = pieces.transpose(1, 0, 2).reshape(mine // n_ch, n_ctx * length)
    return lax.all_gather(pieces, "ch", axis=0, tiled=True)


def ctx_id(index):
    return (index, lax.axis_index("ch"))


def ch_id(index):
    return (lax.axis_index("ctx"), index)


def remote(src, dst, send, recv, device):
    return pltpu.make_async_remote_copy(
        src_ref=src, dst_ref=dst, send_sem=send, recv_sem=recv, device_id=device, device_id_type=MESH
    )


def greet(devices):
    barrier = pltpu.get_barrier_semaphore()
    for device in devices:
        pl.semaphore_signal(barrier, inc=1, device_id=device, device_id_type=MESH)
    pl.semaphore_wait(barrier, len(devices))


def split(wide):
    high = wide.astype(jnp.bfloat16)
    return high, (wide - high.astype(jnp.float32)).astype(jnp.bfloat16)


def dot(a, b, dims):
    return lax.dot_general(a, b, (dims, ((), ())), preferred_element_type=jnp.float32)


def dot_split(a, b, dims):
    return dot(a[0], b[0], dims) + dot(a[0], b[1], dims) + dot(a[1], b[0], dims)


NN = ((1,), (0,))
NT = ((1,), (1,))


def stacked_left(states):
    high, low = split(states)
    high, low = high.astype(jnp.float32), low.astype(jnp.float32)
    return jnp.concatenate([high, low, high], axis=0).T.astype(jnp.bfloat16)


def stacked_right(maps):
    high, low = split(maps)
    return jnp.concatenate([high, high, low], axis=0)


def column(row):
    n = row.shape[1]
    same = lax.broadcasted_iota(jnp.int32, (n, n), 0) == lax.broadcasted_iota(jnp.int32, (n, n), 1)
    return jnp.sum(jnp.where(same, jnp.broadcast_to(row, (n, n)), 0.0), axis=1, keepdims=True)


def fused_kernel(
    docs_ref, decay_ref, residue_ref, query_hbm, key_hbm, value_hbm, weight_hbm, cot_hbm,
    query_grad_hbm, key_grad_hbm, value_grad_hbm, weight_grad_hbm,
    query, key, value, cot, cots, weights, partial, arrived, across_out, across_in,
    kernel_high, kernel_low, mixed_high, mixed_low, filtered_ref, gated_ref, turned, passing, rows_ref,
    grads, acc, half_out, half_in, part_ref, twin_part, slots, joint, back_part, back_twin, back_slots, back_joint, total,
    in_maps, back_maps,
    part_sem, load_sem, weight_sem, store_sem, own_sem,
    z_send, z_recv, half_send, half_recv,
    far_send, far_recv, across_send, across_recv,
    s_send, s_recv, sz_send, sz_recv, b_send, b_recv, bz_send, bz_recv,
    turn_send, turn_recv, join_send, join_recv, wide_send, wide_recv,
):
    f32, bf16 = jnp.float32, jnp.bfloat16
    me, ch = lax.axis_index("ctx"), lax.axis_index("ch")
    z, x = me // 2, me % 2
    twin = me + 1 - 2 * x
    y, core = ch // 2, ch % 2
    across = (1 - y) * 2 + core
    mate = y * 2 + 1 - core
    far = (1 - y) * 2 + 1 - core
    length, width = cot.shape
    rows_all = query.shape[0]
    half_rows = rows_all // 2
    piece = turned.shape[1]
    poles = part_ref.shape[1]
    part_width = width // PARTS

    parts = [pl.ds(p * part_width, part_width) for p in range(PARTS)]
    part_loads = [
        pltpu.make_async_copy(cot_hbm.at[:, parts[p]], cots.at[z, p], part_sem.at[p]) for p in range(PARTS)
    ]
    for copy in part_loads:
        copy.start()

    greet(
        [ctx_id(twin)]
        + [ctx_id(lax.rem(me + 2 * d, 8)) for d in range(1, 4)]
        + [ch_id(lax.rem(ch + d, 4)) for d in range(1, 4)]
    )

    def goes(side):
        return z < 3 if side > 0 else z > 0

    def along(origin, side, p):
        to = cots.at[origin, p]
        return remote(to, to, z_send.at[(side + 1) // 2, p, origin], z_recv.at[p, origin], ctx_id(me + 2 * side))

    def members(quarter):
        return range(quarter * PARTS // 4, (quarter + 1) * PARTS // 4)

    def own_along(quarter):
        for p in members(quarter):
            part_loads[p].wait()
            for side in (1, -1):

                @pl.when(goes(side))
                def _():
                    along(z, side, p).start()

    own_along(0)

    loads = [
        pltpu.make_async_copy(src, to, load_sem.at[k])
        for k, (src, to) in enumerate(((cot_hbm, cot), (key_hbm, key), (value_hbm, value), (query_hbm, query)))
    ]
    weight_loads = [
        pltpu.make_async_copy(
            weight_hbm.at[pl.ds(pl.multiple_of(index * rows_all, rows_all), rows_all)], weights.at[k], weight_sem.at[k]
        )
        for k, index in enumerate((far, across, mate, ch))
    ]
    for copy in [loads[0], weight_loads[0]] + loads[1:3] + [weight_loads[1], loads[3]] + weight_loads[2:]:
        copy.start()
    own_along(1)

    def step(s, quarter):
        for p in members(quarter):
            for side in (1, -1):
                origin = z - side * s

                @pl.when((origin >= 0) & (origin <= 3))
                def _():
                    along(origin, side, p).wait_recv()

                    @pl.when(goes(side))
                    def _():
                        along(origin, side, p).start()

    def doc_at(position):
        count = jnp.int32(0)
        for k in range(docs_ref.shape[0]):
            count = count + jnp.where(docs_ref[k] <= position, 1, 0)
        return count

    start = me * length
    last = doc_at(start + length - 1)
    previous = jnp.where(me > 0, doc_at(start - 1), -1)

    def docs_of(offsets):
        count = jnp.zeros(offsets.shape, jnp.int32)
        for k in range(docs_ref.shape[0]):
            count = count + jnp.where(docs_ref[k] <= offsets + start, 1, 0)
        return count

    lanes = lax.broadcasted_iota(jnp.int32, (1, length), 1)
    ids_row = docs_of(lanes)
    ids_column = docs_of(lax.broadcasted_iota(jnp.int32, (length, 1), 0))
    alive = jnp.where(ids_row == previous, 1.0, 0.0)
    tail = jnp.where(ids_row == last, 1.0, 0.0)
    place = lanes.astype(f32)
    rates = [column(decay_ref[pl.ds(g, 1), :]) for g in range(2)]
    gains = [column(residue_ref[pl.ds(g, 1), :]) for g in range(2)]

    tile = TILE
    shift = 0.5 * tile
    near_place = lax.broadcasted_iota(jnp.int32, (1, tile), 1).astype(f32)
    causal_rows = lax.broadcasted_iota(jnp.int32, (length, tile), 0)
    causal_columns = lax.broadcasted_iota(jnp.int32, (length, tile), 1)
    out_maps, adjoint_maps = [], []
    for g in range(2):
        rate, gain = rates[g], gains[g]
        rising = gain * jnp.exp(-rate * (place - shift))
        falling = jnp.exp(rate * (near_place - shift))
        strip = dot(stacked_left(rising), stacked_right(falling), NN)
        for b in range(length // tile):
            s0 = b * tile
            columns = pl.ds(s0, tile)
            same = (causal_rows[: length - s0] >= causal_columns[: length - s0]) & (
                ids_column[s0:] == ids_row[:, s0 : s0 + tile]
            )
            high, low = split(jnp.where(same, strip[: length - s0], 0.0))
            kernel_high[g, pl.ds(s0, length - s0), columns] = high
            kernel_low[g, pl.ds(s0, length - s0), columns] = low
            if b > 0:
                kernel_high[g, pl.ds(0, s0), columns] = jnp.zeros((s0, tile), bf16)
                kernel_low[g, pl.ds(0, s0), columns] = jnp.zeros((s0, tile), bf16)
        out_maps.append(split(jnp.exp(-rate * (length - 1.0 - place)) * tail))
        adjoint_maps.append(split(jnp.exp(-rate * place) * alive))
        in_maps[g] = stacked_right(gain * jnp.exp(-rate * (place + 1.0)) * alive)
        back_maps[g] = stacked_right(gain * jnp.exp(-rate * (length - place)) * tail)

    def multiply(k, store):
        weight_loads[k].wait()

        @pl.loop(0, 4)
        def _(r):
            rows = pl.ds(pl.multiple_of(r * 2 * piece, piece), 2 * piece)
            store(rows, dot(weights[k, rows, :], cot[...], NT))

    def to_partial(k):
        def store(rows, product):
            partial[k, rows, :] = product

        return store

    to_mate = [
        remote(partial.at[k], arrived.at[k], far_send.at[k], far_recv.at[k], ch_id(mate)) for k in range(2)
    ]
    loads[0].wait()
    multiply(0, to_partial(0))
    to_mate[0].start()

    loads[1].wait()
    loads[2].wait()

    @pl.loop(0, 8)
    def _(r):
        rows = pl.ds(pl.multiple_of(r * piece, piece), piece)
        high, low = split(key[rows, :].astype(f32) * value[rows, :].astype(f32))
        mixed_high[rows, :] = high
        mixed_low[rows, :] = low

    def state_of(g, maps):
        rows = pl.ds(g * half_rows, half_rows)
        return dot_split(maps, (mixed_high[rows, :], mixed_low[rows, :]), NT)

    for g in range(2):
        part_ref[g] = state_of(g, out_maps[g])
    to_twin_state = remote(part_ref, twin_part, s_send, s_recv, ctx_id(twin))
    to_twin_state.start()

    chunks = [pl.ds(r * 2 * piece, 2 * piece) for r in range(4)]
    across_copies = [
        remote(across_out.at[rows], across_in.at[rows], across_send.at[r], across_recv.at[r], ch_id(across))
        for r, rows in enumerate(chunks)
    ]
    weight_loads[1].wait()
    to_mate[0].wait_recv()
    for r, rows in enumerate(chunks):
        summed = dot(weights[1, rows, :], cot[...], NT) + arrived[0, rows, :]
        across_out[rows, :] = summed.astype(bf16)
        if r < 2:
            across_copies[r].start()

    first_half = jnp.where(x == 0, 1.0, 0.0)
    second_half = 1.0 - first_half
    plane_first = doc_at((2 * z + 1) * length - 1)
    plane_last = doc_at((2 * z + 2) * length - 1)
    plane_before = jnp.where(z > 0, doc_at(2 * z * length - 1), -1)
    first_whole = jnp.where(plane_first == plane_before, 1.0, 0.0)
    second_whole = jnp.where(plane_first == plane_last, 1.0, 0.0)
    decays = [jnp.exp(-rates[g] * float(length)) for g in range(2)]

    to_twin_state.wait_recv()
    for g in range(2):
        through = decays[g] * second_whole
        joint[g] = part_ref[g] * (first_half * through + second_half) + twin_part[g] * (
            first_half + second_half * through
        )

    def state_sends(sign, src, to_slots, send, recv):
        copies = []
        for d in range(1, 4):
            to, came = z + sign * d, z - sign * d
            out = remote(src, to_slots.at[z], send.at[d], recv.at[d], ctx_id(me + 2 * sign * d))
            back = remote(src, to_slots.at[came], send.at[d], recv.at[d], ctx_id(me - 2 * sign * d))
            copies.append(((to >= 0) & (to <= 3), out, (came >= 0) & (came <= 3), came, back))
        for there, out, _, _, _ in reversed(copies):

            @pl.when(there)
            def _():
                out.start()

        return copies

    def gather_states(copies, sign, from_slots):
        total[...] = jnp.zeros_like(total)
        edge = plane_before if sign > 0 else plane_last
        for _, _, there, came, back in copies:

            @pl.when(there)
            def _():
                back.wait_recv()
                other = doc_at((2 * came + 2) * length - 1) if sign > 0 else doc_at(2 * came * length - 1)
                weight = jnp.where(other == edge, 1.0, 0.0)
                between = (z - 1 - came) if sign > 0 else (came - 1 - z)
                distance = (2 * length * between).astype(f32)
                for g in range(2):
                    total[g] += from_slots[came, g] * (jnp.exp(-rates[g] * distance) * weight)

    states_ahead = state_sends(1, joint, slots, sz_send, sz_recv)

    own_along(2)

    for g in range(2):

        @pl.loop(0, 2)
        def _(r):
            rows = pl.ds(pl.multiple_of(g * half_rows + r * 2 * piece, piece), 2 * piece)
            filtered_ref[rows, :] = dot_split(
                (mixed_high[rows, :], mixed_low[rows, :]), (kernel_high[g], kernel_low[g]), NT
            )

    multiply(2, to_partial(1))
    to_mate[1].start()
    own_along(3)
    multiply(3, to_partial(2))

    @pl.when(z >= 2)
    def _():
        across_copies[2].start()

    step(1, 0)
    step(1, 1)
    loads[3].wait()
    gather_states(states_ahead, 1, slots)

    for g in range(2):
        entering = total[g] * (first_half + second_half * decays[g] * first_whole) + twin_part[g] * second_half
        carried = stacked_left(entering)
        for r in range(4):
            rows = pl.ds(g * half_rows + r * piece, piece)
            filtered = filtered_ref[rows, :] + dot(carried[r * piece : (r + 1) * piece], in_maps[g], NN)
            filtered_ref[rows, :] = filtered
            gated_ref[g, r] = (query[rows, :].astype(f32) * filtered).astype(bf16)

    turns = []
    for d in range(1, 4):
        to = lax.rem(ch + d, 4)
        came = lax.rem(ch + 4 - d, 4)
        for h in range(2):
            slot = 2 * d + h
            out = remote(gated_ref.at[h, to], turned.at[2 * ch + h], turn_send.at[slot], turn_recv.at[slot], ch_id(to))
            out.start()
            back = remote(
                gated_ref.at[h, to], turned.at[2 * came + h], turn_send.at[slot], turn_recv.at[slot], ch_id(to)
            )
            turns.append((out, back))
    own_turns = [pltpu.make_async_copy(gated_ref.at[h, ch], turned.at[2 * ch + h], own_sem.at[h]) for h in range(2)]
    for copy in own_turns:
        copy.start()
    @pl.when(z < 2)
    def _():
        across_copies[2].start()

    across_copies[3].start()

    for copy in own_turns:
        copy.wait()
    for out, back in turns:
        back.wait_recv()

    def hop(origin, to, side, a, b):
        src = turned.at[pl.ds(2 * to, 2)] if a == 0 else passing.at[origin, to]
        dst = rows_ref.at[origin, ch] if b == 1 else passing.at[origin, to]
        return remote(
            src, dst, join_send.at[(side + 1) // 2, a, b], join_recv.at[origin, to], ctx_id(me + 2 * side)
        )

    def hops(a):
        for b in range(3 - a, 0, -1):
            for side in (1, -1):
                origin, to = z - side * a, z + side * b
                yield (origin >= 0) & (origin <= 3) & (to >= 0) & (to <= 3), origin, to, side, b

    def pass_on(a):
        for there, origin, to, side, b in hops(a):

            @pl.when(there)
            def _():
                if a > 0:
                    block = passing.at[origin, to]
                    remote(
                        block, block, join_send.at[0, a, b], join_recv.at[origin, to], ctx_id(me - 2 * side)
                    ).wait_recv()
                hop(origin, to, side, a, b).start()

    pass_on(0)
    own_join = pltpu.make_async_copy(
        turned.at[pl.ds(2 * z, 2)], rows_ref.at[z, ch], own_sem.at[2]
    )
    own_join.start()

    middle = (z * (3 - z)) // 2
    way = 1 - 2 * (z // 2)
    order = [z + way * (k - middle * c) for k, c in enumerate((0, 2, 1, 1))]

    def wide(slot, k, owner, to):
        block = rows_ref.at[order[k], owner]
        return remote(block, block, wide_send.at[slot, k], wide_recv.at[slot, k], ch_id(to))

    def wide_start(k):
        if k == 0:
            own_join.wait()
        else:
            source = order[k]
            block = rows_ref.at[source, ch]
            remote(block, block, join_send.at[0, 0, 1], join_recv.at[source, z], ctx_id(2 * source + x)).wait_recv()
        wide(0, k, ch, across).start()
        wide(1, k, ch, mate).start()

    def wide_on(k):
        wide(0, k, across, across).wait_recv()
        wide(2, k, across, mate).start()

    wide_start(0)
    pass_on(1)
    wide_start(1)
    step(1, 2)
    pass_on(2)
    wide_start(2)
    step(1, 3)
    step(2, 0)

    to_mate[1].wait_recv()
    for copy in across_copies:
        copy.wait_recv()

    @pl.loop(0, 8)
    def _(r):
        rows = pl.ds(pl.multiple_of(r * piece, piece), piece)
        output_grad = partial[2, rows, :] + arrived[1, rows, :] + across_in[rows, :].astype(f32)
        high, low = split(output_grad * query[rows, :].astype(f32))
        mixed_high[rows, :] = high
        mixed_low[rows, :] = low
        grads[0, rows, :] = (output_grad * filtered_ref[rows, :]).astype(bf16)

    for g in range(2):
        back_part[g] = state_of(g, adjoint_maps[g])
    back_twin_state = remote(back_part, back_twin, b_send, b_recv, ctx_id(twin))
    back_twin_state.start()
    stores = [
        pltpu.make_async_copy(grads.at[k], to, store_sem.at[k])
        for k, to in enumerate((query_grad_hbm, key_grad_hbm, value_grad_hbm))
    ]
    stores[0].start()
    wide_on(0)
    step(2, 1)
    wide_start(3)
    wide_on(1)

    back_twin_state.wait_recv()
    for g in range(2):
        through = decays[g] * first_whole
        back_joint[g] = back_part[g] * (second_half * through + first_half) + back_twin[g] * (
            second_half + first_half * through
        )
    states_back = state_sends(-1, back_joint, back_slots, bz_send, bz_recv)

    for g in range(2):

        @pl.loop(0, 2)
        def _(r):
            rows = pl.ds(pl.multiple_of(g * half_rows + r * 2 * piece, piece), 2 * piece)
            filtered_ref[rows, :] = dot_split(
                (mixed_high[rows, :], mixed_low[rows, :]), (kernel_high[g], kernel_low[g]), NN
            )

    step(2, 2)
    wide_on(2)

    norm_factor = 1.0 / math.sqrt(8 * length)

    def product(k, half, p):
        return dot(rows_ref[order[k], :, half].reshape(half_rows, length), cots[order[k], p], NN)

    def add(k):
        wide(1, k, mate, mate).wait_recv()
        wide(2, k, far, mate).wait_recv()

        @pl.loop(0, PARTS)
        def _(p):
            term = product(k, 1 - x, p)
            acc[1 - x, p] = term if k == 0 else acc[1 - x, p] + term

    add(0)
    step(2, 3)
    wide_on(3)

    add(1)
    add(2)
    wide(1, 3, mate, mate).wait_recv()
    wide(2, 3, far, mate).wait_recv()
    halves = [
        remote(half_out.at[p], half_in.at[p], half_send.at[p], half_recv.at[p], ctx_id(twin))
        for p in range(PARTS)
    ]
    store_acc = [
        pltpu.make_async_copy(acc.at[x, p], weight_grad_hbm.at[:, parts[p]], store_sem.at[3 + p])
        for p in range(PARTS)
    ]

    for p in range(PARTS):

        @pl.when(middle == 0)
        def _():
            along(order[3], 1, p).wait_recv()

        half_out[p] = ((acc[1 - x, p] + product(3, 1 - x, p)) * norm_factor).astype(bf16)
        halves[p].start()

    gather_states(states_back, -1, back_slots)
    for g in range(2):
        returning = total[g] * (second_half + first_half * decays[g] * second_whole) + back_twin[g] * first_half
        carried = stacked_left(returning)
        for r in range(4):
            rows = pl.ds(g * half_rows + r * piece, piece)
            spread = filtered_ref[rows, :] + dot(carried[r * piece : (r + 1) * piece], back_maps[g], NN)
            grads[1, rows, :] = (spread * value[rows, :].astype(f32)).astype(bf16)
            grads[2, rows, :] = (spread * key[rows, :].astype(f32)).astype(bf16)
    stores[1].start()
    stores[2].start()

    for p in range(PARTS):
        own = product(0, x, p)
        for k in range(1, 4):
            own += product(k, x, p)
        halves[p].wait_recv()
        acc[x, p] = own * norm_factor + half_in[p].astype(f32)
        store_acc[p].start()

    for origin in range(4):
        for side in (1, -1):

            @pl.when(goes(side) & (origin <= z if side > 0 else origin >= z))
            def _():
                for p in range(PARTS):
                    along(origin, side, p).wait_send()

    for copies in (states_ahead, states_back):
        for there, out, _, _, _ in copies:

            @pl.when(there)
            def _():
                out.wait_send()

    for copy in to_mate + across_copies + [to_twin_state, back_twin_state] + halves:
        copy.wait_send()
    for a in range(3):
        for there, origin, to, side, b in hops(a):

            @pl.when(there)
            def _():
                hop(origin, to, side, a, b).wait_send()

    for out, back in turns:
        out.wait_send()
    for k in range(4):
        wide(0, k, ch, across).wait_send()
        wide(1, k, ch, mate).wait_send()
        wide(2, k, across, mate).wait_send()
    for copy in stores + store_acc:
        copy.wait()


def fused(query_input, key_input, value_input, decay_rate, residue, doc_ends, out_weight, out_cotangent):
    rows, length = query_input.shape
    width = out_cotangent.shape[1]
    groups, poles = decay_rate.shape
    n_ctx, n_ch = lax.axis_size("ctx"), lax.axis_size("ch")
    piece = rows // 2 // n_ch
    anywhere = pl.BlockSpec(memory_space=pl.ANY)
    vmem = pl.BlockSpec(memory_space=pltpu.VMEM)
    smem = pl.BlockSpec(memory_space=pltpu.SMEM)
    f32, bf16 = jnp.float32, jnp.bfloat16
    dma = pltpu.SemaphoreType.DMA
    state = (groups, poles, rows // groups)
    maps = (groups, 3 * poles, length)
    block = (rows, length)
    return pl.pallas_call(
        fused_kernel,
        out_shape=tuple(jax.ShapeDtypeStruct(block, bf16) for _ in range(3))
        + (jax.ShapeDtypeStruct((rows // 2, width), f32),),
        in_specs=[smem, vmem, vmem] + [anywhere] * 5,
        out_specs=(anywhere,) * 4,
        scratch_shapes=[
            pltpu.VMEM(block, bf16), pltpu.VMEM(block, bf16), pltpu.VMEM(block, bf16),
            pltpu.VMEM((length, width), bf16),
            pltpu.VMEM((4, PARTS, length, width // PARTS), bf16),
            pltpu.VMEM((n_ch, rows, width), bf16),
            pltpu.VMEM((3,) + block, f32),
            pltpu.VMEM((2,) + block, f32),
            pltpu.VMEM(block, bf16), pltpu.VMEM(block, bf16),
            pltpu.VMEM((groups, length, length), bf16), pltpu.VMEM((groups, length, length), bf16),
            pltpu.VMEM(block, bf16), pltpu.VMEM(block, bf16),
            pltpu.VMEM(block, f32),
            pltpu.VMEM((2, n_ch, piece, length), bf16),
            pltpu.VMEM((n_ctx, piece, length), bf16),
            pltpu.VMEM((4, 4, 2, piece, length), bf16),
            pltpu.VMEM((4, n_ch, 2, piece, length), bf16),
            pltpu.VMEM((3,) + block, bf16),
            pltpu.VMEM((2, PARTS, rows // 2, width // PARTS), f32),
            pltpu.VMEM((PARTS, rows // 2, width // PARTS), bf16), pltpu.VMEM((PARTS, rows // 2, width // PARTS), bf16),
            pltpu.VMEM(state, f32), pltpu.VMEM(state, f32), pltpu.VMEM((4,) + state, f32), pltpu.VMEM(state, f32),
            pltpu.VMEM(state, f32), pltpu.VMEM(state, f32), pltpu.VMEM((4,) + state, f32), pltpu.VMEM(state, f32),
            pltpu.VMEM(state, f32),
            pltpu.VMEM(maps, bf16), pltpu.VMEM(maps, bf16),
            dma((PARTS,)), dma((4,)), dma((4,)), dma((3 + PARTS,)), dma((3,)),
            dma((2, PARTS, 4)), dma((PARTS, 4)), dma((PARTS,)), dma((PARTS,)),
            dma((2,)), dma((2,)), dma((4,)), dma((4,)),
            dma(()), dma(()), dma((4,)), dma((4,)), dma(()), dma(()), dma((4,)), dma((4,)),
            dma((8,)), dma((8,)), dma((2, 3, 4)), dma((4, 4)), dma((3, 4)), dma((3, 4)),
        ],
        compiler_params=pltpu.CompilerParams(
            collective_id=0, has_side_effects=True, vmem_limit_bytes=VMEM_LIMIT
        ),
        cost_estimate=pl.CostEstimate(flops=10_000_000_000, bytes_accessed=30_000_000, transcendentals=100_000),
        name="fused",
    )(doc_ends, decay_rate, residue, query_input, key_input, value_input, out_weight, out_cotangent)


def move_by_collectives(cotangent, weight, part, near, query, ahead, behind, in_map, out_map):
    n_ctx, n_ch = lax.axis_size("ctx"), lax.axis_size("ch")
    groups = part.shape[0]
    rows, length = query.shape
    query_f = query.astype(jnp.float32)
    cots = lax.all_gather(cotangent, "ctx", axis=0, tiled=True)
    partial_grad = lax.dot_general(
        weight, cotangent, (((1,), (1,)), ((), ())), preferred_element_type=jnp.float32
    )
    output_grad = lax.psum_scatter(partial_grad, "ch", scatter_dimension=0, tiled=True)
    entering = jnp.sum(ahead * lax.all_gather(part, "ctx", axis=0), axis=0)
    carried = jnp.einsum("gnc,gnt->gct", entering, in_map, precision=HIGH).reshape(rows, length)
    filtered = near + carried
    gathered = exchange_rows((query_f * filtered).astype(jnp.bfloat16), n_ctx, n_ch)
    signal = output_grad * query_f
    back_part = jnp.einsum("gnl,gcl->gnc", out_map, signal.reshape(groups, rows // groups, length), precision=HIGH)
    returning = jnp.sum(behind * lax.all_gather(back_part, "ctx", axis=0), axis=0)
    query_grad = (output_grad * filtered).astype(jnp.bfloat16)
    return signal, query_grad, returning, gathered, cots


def local(
    query_input, key_input, value_input, decay_rate, residue, doc_ends, out_weight, out_cotangent
):
    rows_here, length = query_input.shape
    n_ctx, n_ch = lax.axis_size("ctx"), lax.axis_size("ch")
    groups = decay_rate.shape[0]
    if (n_ctx, n_ch, groups) == (8, 4, 2) and rows_here == 1024 and length == 512:
        return fused(
            query_input, key_input, value_input, decay_rate, residue, doc_ends, out_weight, out_cotangent
        )
    group_rows = rows_here // groups
    me = lax.axis_index("ctx")
    offsets = jnp.arange(length, dtype=jnp.int32)
    place = offsets.astype(jnp.float32)
    doc_ids = doc_of(doc_ends, me * length + offsets)
    blocks = jnp.arange(n_ctx, dtype=jnp.int32)
    last_ids = doc_of(doc_ends, (blocks + 1) * length - 1)
    previous = jnp.where(me > 0, jnp.sum((doc_ends <= me * length - 1).astype(jnp.int32)), -1)
    last = doc_ids[-1]

    alive_mask = (doc_ids == previous).astype(jnp.float32)
    tail_mask = (doc_ids == last).astype(jnp.float32)
    rate = decay_rate[:, :, None]
    carry_in_map = residue[:, :, None] * jnp.exp(-rate * (place + 1.0)) * alive_mask
    carry_out_map = jnp.exp(-rate * (length - 1.0 - place)) * tail_mask
    back_out_map = jnp.exp(-rate * place) * alive_mask
    back_in_map = residue[:, :, None] * jnp.exp(-rate * (length - place)) * tail_mask
    steps_ahead = me - 1 - blocks
    joined_ahead = (steps_ahead >= 0) & (last_ids == previous)
    ahead_weight = jnp.where(
        joined_ahead[:, None, None],
        jnp.exp(-decay_rate[None] * (length * jnp.maximum(steps_ahead, 0)).astype(jnp.float32)[:, None, None]),
        0.0,
    )
    steps_back = blocks - 1 - me
    before_ids = jnp.concatenate([jnp.full((1,), -1, jnp.int32), last_ids[:-1]])
    joined_back = (steps_back >= 0) & (before_ids == last)
    back_weight = jnp.where(
        joined_back[:, None, None],
        jnp.exp(-decay_rate[None] * (length * jnp.maximum(steps_back, 0)).astype(jnp.float32)[:, None, None]),
        0.0,
    )

    key_f = key_input.astype(jnp.float32)
    value_f = value_input.astype(jnp.float32)
    mixed = (key_f * value_f).reshape(groups, group_rows, length)
    forward_part = jnp.einsum("gnl,gcl->gnc", carry_out_map, mixed, precision=HIGH)
    kernel = local_kernel(decay_rate, residue, doc_ids, length)
    near = jnp.einsum("gcs,gts->gct", mixed, kernel, precision=HIGH).reshape(rows_here, length)
    wide = (n_ctx,) + forward_part.shape
    signal, query_grad, returning, gated_rows, cotangent_all = move_by_collectives(
        out_cotangent,
        out_weight,
        forward_part,
        near,
        query_input,
        jnp.broadcast_to(ahead_weight[..., None], wide),
        jnp.broadcast_to(back_weight[..., None], wide),
        carry_in_map,
        back_out_map,
    )
    signal = signal.reshape(groups, group_rows, length)
    spread = jnp.einsum("gct,gts->gcs", signal, kernel, precision=HIGH)
    spread = spread + jnp.einsum("gnc,gns->gcs", returning, back_in_map, precision=HIGH)
    spread = spread.reshape(rows_here, length)
    key_grad = (spread * value_f).astype(jnp.bfloat16)
    value_grad = (spread * key_f).astype(jnp.bfloat16)

    norm_factor = 1.0 / math.sqrt(length * n_ctx)
    weight_grad = jnp.dot(gated_rows, cotangent_all, preferred_element_type=jnp.float32) * norm_factor
    return (query_grad, key_grad, value_grad, weight_grad)


def solution(mesh):
    return jax.shard_map(
        local,
        mesh=mesh,
        in_specs=(
            P("ch", "ctx"),
            P("ch", "ctx"),
            P("ch", "ctx"),
            P("ch", None),
            P("ch", None),
            P(),
            P(None, "ch"),
            P("ctx", "ch"),
        ),
        out_specs=(P("ch", "ctx"), P("ch", "ctx"), P("ch", "ctx"), P("ctx", "ch")),
        check_vma=False,
    )
```

```python
import functools
import math

import jax
import jax.numpy as jnp
from jax import lax
from jax.experimental import pallas as pl
from jax.experimental.pallas import tpu as pltpu
from jax.sharding import PartitionSpec as P

MESH = pl.DeviceIdType.MESH
HIGH = lax.Precision.HIGH
TILE = 128
PARTS = 4
VMEM_LIMIT = 60 * 1024 * 1024


def doc_of(doc_ends, positions):
    return jnp.sum((doc_ends[None, :] <= positions[:, None]).astype(jnp.int32), axis=1)


def local_kernel(decay_rate, residue, doc_ids, length):
    groups = decay_rate.shape[0]
    place = jnp.arange(length, dtype=jnp.float32)
    narrow = jnp.arange(TILE, dtype=jnp.float32)
    half = 0.5 * TILE
    rising = jnp.exp(-decay_rate[:, None, :] * (place - half)[None, :, None]) * residue[:, None, :]
    falling = jnp.exp(decay_rate[:, None, :] * (narrow - half)[None, :, None])
    strip = jnp.einsum("gtn,gsn->gts", rising, falling, precision=lax.Precision.HIGHEST)
    columns = []
    for start in range(0, length, TILE):
        top = jnp.zeros((groups, start, TILE), jnp.float32)
        columns.append(jnp.concatenate([top, strip[:, : length - start]], axis=1))
    kernel = jnp.concatenate(columns, axis=2)
    offsets = jnp.arange(length, dtype=jnp.int32)
    causal = (offsets[:, None] >= offsets[None, :]) & (doc_ids[:, None] == doc_ids[None, :])
    return jnp.where(causal[None], kernel, 0.0)


def exchange_rows(gated, n_ctx, n_ch):
    rows, length = gated.shape
    mine = rows * n_ch // n_ctx
    pieces = gated.reshape(n_ctx // n_ch, n_ch, mine // n_ch, length)
    pieces = lax.all_to_all(pieces, "ch", split_axis=1, concat_axis=0, tiled=True)
    pieces = pieces.reshape(n_ctx, mine // n_ch, length)
    pieces = lax.all_to_all(pieces, "ctx", split_axis=0, concat_axis=0, tiled=True)
    pieces = pieces.transpose(1, 0, 2).reshape(mine // n_ch, n_ctx * length)
    return lax.all_gather(pieces, "ch", axis=0, tiled=True)


def ctx_id(index):
    return (index, lax.axis_index("ch"))


def ch_id(index):
    return (lax.axis_index("ctx"), index)


def remote(src, dst, send, recv, device):
    return pltpu.make_async_remote_copy(
        src_ref=src, dst_ref=dst, send_sem=send, recv_sem=recv, device_id=device, device_id_type=MESH
    )


def greet(devices):
    barrier = pltpu.get_barrier_semaphore()
    for device in devices:
        pl.semaphore_signal(barrier, inc=1, device_id=device, device_id_type=MESH)
    pl.semaphore_wait(barrier, len(devices))


def split(wide):
    high = wide.astype(jnp.bfloat16)
    return high, (wide - high.astype(jnp.float32)).astype(jnp.bfloat16)


def dot(a, b, dims):
    return lax.dot_general(a, b, (dims, ((), ())), preferred_element_type=jnp.float32)


def dot_split(a, b, dims):
    return dot(a[0], b[0], dims) + dot(a[0], b[1], dims) + dot(a[1], b[0], dims)


NN = ((1,), (0,))
NT = ((1,), (1,))


def stacked_left(states):
    high, low = split(states)
    high, low = high.astype(jnp.float32), low.astype(jnp.float32)
    return jnp.concatenate([high, low, high], axis=0).T.astype(jnp.bfloat16)


def stacked_right(maps):
    high, low = split(maps)
    return jnp.concatenate([high, high, low], axis=0)


def column(row):
    n = row.shape[1]
    same = lax.broadcasted_iota(jnp.int32, (n, n), 0) == lax.broadcasted_iota(jnp.int32, (n, n), 1)
    return jnp.sum(jnp.where(same, jnp.broadcast_to(row, (n, n)), 0.0), axis=1, keepdims=True)


def fused_kernel(
    docs_ref, decay_ref, residue_ref, query_hbm, key_hbm, value_hbm, weight_hbm, cot_hbm,
    query_grad_hbm, key_grad_hbm, value_grad_hbm, weight_grad_hbm,
    query, key, value, cot, cots, weights, partial, arrived, across_out, across_in,
    kernel_high, kernel_low, mixed_high, mixed_low, filtered_ref, gated_ref, turned, passing, rows_ref,
    grads, acc, half_out, half_in, part_ref, twin_part, slots, joint, back_part, back_twin, back_slots, back_joint, total,
    in_maps, back_maps,
    part_sem, load_sem, weight_sem, store_sem, own_sem,
    z_send, z_recv, half_send, half_recv,
    far_send, far_recv, across_send, across_recv,
    s_send, s_recv, sz_send, sz_recv, b_send, b_recv, bz_send, bz_recv,
    turn_send, turn_recv, join_send, join_recv, wide_send, wide_recv,
):
    f32, bf16 = jnp.float32, jnp.bfloat16
    me, ch = lax.axis_index("ctx"), lax.axis_index("ch")
    z, x = me // 2, me % 2
    twin = me + 1 - 2 * x
    y, core = ch // 2, ch % 2
    across = (1 - y) * 2 + core
    mate = y * 2 + 1 - core
    far = (1 - y) * 2 + 1 - core
    length, width = cot.shape
    rows_all = query.shape[0]
    half_rows = rows_all // 2
    piece = turned.shape[1]
    poles = part_ref.shape[1]
    part_width = width // PARTS

    parts = [pl.ds(p * part_width, part_width) for p in range(PARTS)]
    part_loads = [
        pltpu.make_async_copy(cot_hbm.at[:, parts[p]], cots.at[z, p], part_sem.at[p]) for p in range(PARTS)
    ]
    for copy in part_loads:
        copy.start()

    greet(
        [ctx_id(twin)]
        + [ctx_id(lax.rem(me + 2 * d, 8)) for d in range(1, 4)]
        + [ch_id(lax.rem(ch + d, 4)) for d in range(1, 4)]
    )

    def goes(side):
        return z < 3 if side > 0 else z > 0

    def along(origin, side, p):
        to = cots.at[origin, p]
        return remote(to, to, z_send.at[(side + 1) // 2, p, origin], z_recv.at[p, origin], ctx_id(me + 2 * side))

    def members(quarter):
        return range(quarter * PARTS // 4, (quarter + 1) * PARTS // 4)

    def own_along(quarter):
        for p in members(quarter):
            part_loads[p].wait()
            for side in (1, -1):

                @pl.when(goes(side))
                def _():
                    along(z, side, p).start()

    own_along(0)

    loads = [
        pltpu.make_async_copy(src, to, load_sem.at[k])
        for k, (src, to) in enumerate(((cot_hbm, cot), (key_hbm, key), (value_hbm, value), (query_hbm, query)))
    ]
    weight_loads = [
        pltpu.make_async_copy(
            weight_hbm.at[pl.ds(pl.multiple_of(index * rows_all, rows_all), rows_all)], weights.at[k], weight_sem.at[k]
        )
        for k, index in enumerate((far, across, mate, ch))
    ]
    for copy in [loads[0], weight_loads[0]] + loads[1:3] + [weight_loads[1], loads[3]] + weight_loads[2:]:
        copy.start()
    own_along(1)

    def step(s, quarter):
        for p in members(quarter):
            for side in (1, -1):
                origin = z - side * s

                @pl.when((origin >= 0) & (origin <= 3))
                def _():
                    along(origin, side, p).wait_recv()

                    @pl.when(goes(side))
                    def _():
                        along(origin, side, p).start()

    def doc_at(position):
        count = jnp.int32(0)
        for k in range(docs_ref.shape[0]):
            count = count + jnp.where(docs_ref[k] <= position, 1, 0)
        return count

    start = me * length
    last = doc_at(start + length - 1)
    previous = jnp.where(me > 0, doc_at(start - 1), -1)

    def docs_of(offsets):
        count = jnp.zeros(offsets.shape, jnp.int32)
        for k in range(docs_ref.shape[0]):
            count = count + jnp.where(docs_ref[k] <= offsets + start, 1, 0)
        return count

    lanes = lax.broadcasted_iota(jnp.int32, (1, length), 1)
    ids_row = docs_of(lanes)
    ids_column = docs_of(lax.broadcasted_iota(jnp.int32, (length, 1), 0))
    alive = jnp.where(ids_row == previous, 1.0, 0.0)
    tail = jnp.where(ids_row == last, 1.0, 0.0)
    place = lanes.astype(f32)
    rates = [column(decay_ref[pl.ds(g, 1), :]) for g in range(2)]
    gains = [column(residue_ref[pl.ds(g, 1), :]) for g in range(2)]

    tile = TILE
    shift = 0.5 * tile
    near_place = lax.broadcasted_iota(jnp.int32, (1, tile), 1).astype(f32)
    causal_rows = lax.broadcasted_iota(jnp.int32, (length, tile), 0)
    causal_columns = lax.broadcasted_iota(jnp.int32, (length, tile), 1)
    out_maps, adjoint_maps = [], []
    for g in range(2):
        rate, gain = rates[g], gains[g]
        rising = gain * jnp.exp(-rate * (place - shift))
        falling = jnp.exp(rate * (near_place - shift))
        strip = dot(stacked_left(rising), stacked_right(falling), NN)
        for b in range(length // tile):
            s0 = b * tile
            columns = pl.ds(s0, tile)
            same = (causal_rows[: length - s0] >= causal_columns[: length - s0]) & (
                ids_column[s0:] == ids_row[:, s0 : s0 + tile]
            )
            high, low = split(jnp.where(same, strip[: length - s0], 0.0))
            kernel_high[g, pl.ds(s0, length - s0), columns] = high
            kernel_low[g, pl.ds(s0, length - s0), columns] = low
            if b > 0:
                kernel_high[g, pl.ds(0, s0), columns] = jnp.zeros((s0, tile), bf16)
                kernel_low[g, pl.ds(0, s0), columns] = jnp.zeros((s0, tile), bf16)
        out_maps.append(split(jnp.exp(-rate * (length - 1.0 - place)) * tail))
        adjoint_maps.append(split(jnp.exp(-rate * place) * alive))
        in_maps[g] = stacked_right(gain * jnp.exp(-rate * (place + 1.0)) * alive)
        back_maps[g] = stacked_right(gain * jnp.exp(-rate * (length - place)) * tail)

    def multiply(k, store):
        weight_loads[k].wait()

        @pl.loop(0, 4)
        def _(r):
            rows = pl.ds(pl.multiple_of(r * 2 * piece, piece), 2 * piece)
            store(rows, dot(weights[k, rows, :], cot[...], NT))

    def to_partial(k):
        def store(rows, product):
            partial[k, rows, :] = product

        return store

    to_mate = [
        remote(partial.at[k], arrived.at[k], far_send.at[k], far_recv.at[k], ch_id(mate)) for k in range(2)
    ]
    loads[0].wait()
    multiply(0, to_partial(0))
    to_mate[0].start()

    loads[1].wait()
    loads[2].wait()

    @pl.loop(0, 8)
    def _(r):
        rows = pl.ds(pl.multiple_of(r * piece, piece), piece)
        high, low = split(key[rows, :].astype(f32) * value[rows, :].astype(f32))
        mixed_high[rows, :] = high
        mixed_low[rows, :] = low

    def state_of(g, maps):
        rows = pl.ds(g * half_rows, half_rows)
        return dot_split(maps, (mixed_high[rows, :], mixed_low[rows, :]), NT)

    for g in range(2):
        part_ref[g] = state_of(g, out_maps[g])
    to_twin_state = remote(part_ref, twin_part, s_send, s_recv, ctx_id(twin))
    to_twin_state.start()

    chunks = [pl.ds(r * 2 * piece, 2 * piece) for r in range(4)]
    across_copies = [
        remote(across_out.at[rows], across_in.at[rows], across_send.at[r], across_recv.at[r], ch_id(across))
        for r, rows in enumerate(chunks)
    ]
    weight_loads[1].wait()
    to_mate[0].wait_recv()
    for r, rows in enumerate(chunks):
        summed = dot(weights[1, rows, :], cot[...], NT) + arrived[0, rows, :]
        across_out[rows, :] = summed.astype(bf16)
        if r < 2:
            across_copies[r].start()

    first_half = jnp.where(x == 0, 1.0, 0.0)
    second_half = 1.0 - first_half
    plane_first = doc_at((2 * z + 1) * length - 1)
    plane_last = doc_at((2 * z + 2) * length - 1)
    plane_before = jnp.where(z > 0, doc_at(2 * z * length - 1), -1)
    first_whole = jnp.where(plane_first == plane_before, 1.0, 0.0)
    second_whole = jnp.where(plane_first == plane_last, 1.0, 0.0)
    decays = [jnp.exp(-rates[g] * float(length)) for g in range(2)]

    to_twin_state.wait_recv()
    for g in range(2):
        through = decays[g] * second_whole
        joint[g] = part_ref[g] * (first_half * through + second_half) + twin_part[g] * (
            first_half + second_half * through
        )

    def state_sends(sign, src, to_slots, send, recv):
        copies = []
        for d in range(1, 4):
            to, came = z + sign * d, z - sign * d
            out = remote(src, to_slots.at[z], send.at[d], recv.at[d], ctx_id(me + 2 * sign * d))
            back = remote(src, to_slots.at[came], send.at[d], recv.at[d], ctx_id(me - 2 * sign * d))
            copies.append(((to >= 0) & (to <= 3), out, (came >= 0) & (came <= 3), came, back))
        for there, out, _, _, _ in reversed(copies):

            @pl.when(there)
            def _():
                out.start()

        return copies

    def gather_states(copies, sign, from_slots):
        total[...] = jnp.zeros_like(total)
        edge = plane_before if sign > 0 else plane_last
        for _, _, there, came, back in copies:

            @pl.when(there)
            def _():
                back.wait_recv()
                other = doc_at((2 * came + 2) * length - 1) if sign > 0 else doc_at(2 * came * length - 1)
                weight = jnp.where(other == edge, 1.0, 0.0)
                between = (z - 1 - came) if sign > 0 else (came - 1 - z)
                distance = (2 * length * between).astype(f32)
                for g in range(2):
                    total[g] += from_slots[came, g] * (jnp.exp(-rates[g] * distance) * weight)

    states_ahead = state_sends(1, joint, slots, sz_send, sz_recv)

    own_along(2)

    for g in range(2):

        @pl.loop(0, 2)
        def _(r):
            rows = pl.ds(pl.multiple_of(g * half_rows + r * 2 * piece, piece), 2 * piece)
            filtered_ref[rows, :] = dot_split(
                (mixed_high[rows, :], mixed_low[rows, :]), (kernel_high[g], kernel_low[g]), NT
            )

    multiply(2, to_partial(1))
    to_mate[1].start()
    own_along(3)
    multiply(3, to_partial(2))

    @pl.when(z >= 2)
    def _():
        across_copies[2].start()

    step(1, 0)
    step(1, 1)
    loads[3].wait()
    gather_states(states_ahead, 1, slots)

    for g in range(2):
        entering = total[g] * (first_half + second_half * decays[g] * first_whole) + twin_part[g] * second_half
        carried = stacked_left(entering)
        for r in range(4):
            rows = pl.ds(g * half_rows + r * piece, piece)
            filtered = filtered_ref[rows, :] + dot(carried[r * piece : (r + 1) * piece], in_maps[g], NN)
            filtered_ref[rows, :] = filtered
            gated_ref[g, r] = (query[rows, :].astype(f32) * filtered).astype(bf16)

    turns = []
    for d in range(1, 4):
        to = lax.rem(ch + d, 4)
        came = lax.rem(ch + 4 - d, 4)
        for h in range(2):
            slot = 2 * d + h
            out = remote(gated_ref.at[h, to], turned.at[2 * ch + h], turn_send.at[slot], turn_recv.at[slot], ch_id(to))
            out.start()
            back = remote(
                gated_ref.at[h, to], turned.at[2 * came + h], turn_send.at[slot], turn_recv.at[slot], ch_id(to)
            )
            turns.append((out, back))
    own_turns = [pltpu.make_async_copy(gated_ref.at[h, ch], turned.at[2 * ch + h], own_sem.at[h]) for h in range(2)]
    for copy in own_turns:
        copy.start()
    @pl.when(z < 2)
    def _():
        across_copies[2].start()

    across_copies[3].start()

    for copy in own_turns:
        copy.wait()
    for out, back in turns:
        back.wait_recv()

    def hop(origin, to, side, a, b):
        src = turned.at[pl.ds(2 * to, 2)] if a == 0 else passing.at[origin, to]
        dst = rows_ref.at[origin, ch] if b == 1 else passing.at[origin, to]
        return remote(
            src, dst, join_send.at[(side + 1) // 2, a, b], join_recv.at[origin, to], ctx_id(me + 2 * side)
        )

    def hops(a):
        for b in range(3 - a, 0, -1):
            for side in (1, -1):
                origin, to = z - side * a, z + side * b
                yield (origin >= 0) & (origin <= 3) & (to >= 0) & (to <= 3), origin, to, side, b

    def pass_on(a):
        for there, origin, to, side, b in hops(a):

            @pl.when(there)
            def _():
                if a > 0:
                    block = passing.at[origin, to]
                    remote(
                        block, block, join_send.at[0, a, b], join_recv.at[origin, to], ctx_id(me - 2 * side)
                    ).wait_recv()
                hop(origin, to, side, a, b).start()

    pass_on(0)
    own_join = pltpu.make_async_copy(
        turned.at[pl.ds(2 * z, 2)], rows_ref.at[z, ch], own_sem.at[2]
    )
    own_join.start()

    middle = (z * (3 - z)) // 2
    way = 1 - 2 * (z // 2)
    order = [z + way * (k - middle * c) for k, c in enumerate((0, 2, 1, 1))]

    def wide(slot, k, owner, to):
        block = rows_ref.at[order[k], owner]
        return remote(block, block, wide_send.at[slot, k], wide_recv.at[slot, k], ch_id(to))

    def wide_start(k):
        if k == 0:
            own_join.wait()
        else:
            source = order[k]
            block = rows_ref.at[source, ch]
            remote(block, block, join_send.at[0, 0, 1], join_recv.at[source, z], ctx_id(2 * source + x)).wait_recv()
        wide(0, k, ch, across).start()
        wide(1, k, ch, mate).start()

    def wide_on(k):
        wide(0, k, across, across).wait_recv()
        wide(2, k, across, mate).start()

    wide_start(0)
    pass_on(1)
    wide_start(1)
    pass_on(2)
    wide_start(2)
    step(1, 2)
    step(1, 3)
    step(2, 0)

    to_mate[1].wait_recv()
    for copy in across_copies:
        copy.wait_recv()

    @pl.loop(0, 8)
    def _(r):
        rows = pl.ds(pl.multiple_of(r * piece, piece), piece)
        output_grad = partial[2, rows, :] + arrived[1, rows, :] + across_in[rows, :].astype(f32)
        high, low = split(output_grad * query[rows, :].astype(f32))
        mixed_high[rows, :] = high
        mixed_low[rows, :] = low
        grads[0, rows, :] = (output_grad * filtered_ref[rows, :]).astype(bf16)

    for g in range(2):
        back_part[g] = state_of(g, adjoint_maps[g])
    back_twin_state = remote(back_part, back_twin, b_send, b_recv, ctx_id(twin))
    back_twin_state.start()
    stores = [
        pltpu.make_async_copy(grads.at[k], to, store_sem.at[k])
        for k, to in enumerate((query_grad_hbm, key_grad_hbm, value_grad_hbm))
    ]
    stores[0].start()
    wide_on(0)
    step(2, 1)
    wide_start(3)
    wide_on(1)

    back_twin_state.wait_recv()
    for g in range(2):
        through = decays[g] * first_whole
        back_joint[g] = back_part[g] * (second_half * through + first_half) + back_twin[g] * (
            second_half + first_half * through
        )
    states_back = state_sends(-1, back_joint, back_slots, bz_send, bz_recv)

    for g in range(2):

        @pl.loop(0, 2)
        def _(r):
            rows = pl.ds(pl.multiple_of(g * half_rows + r * 2 * piece, piece), 2 * piece)
            filtered_ref[rows, :] = dot_split(
                (mixed_high[rows, :], mixed_low[rows, :]), (kernel_high[g], kernel_low[g]), NN
            )

    step(2, 2)
    wide_on(2)

    norm_factor = 1.0 / math.sqrt(8 * length)

    def product(k, half, p):
        return dot(rows_ref[order[k], :, half].reshape(half_rows, length), cots[order[k], p], NN)

    def add(k):
        wide(1, k, mate, mate).wait_recv()
        wide(2, k, far, mate).wait_recv()

        @pl.loop(0, PARTS)
        def _(p):
            term = product(k, 1 - x, p)
            acc[1 - x, p] = term if k == 0 else acc[1 - x, p] + term

    add(0)
    step(2, 3)
    wide_on(3)

    add(1)
    add(2)
    wide(1, 3, mate, mate).wait_recv()
    wide(2, 3, far, mate).wait_recv()
    halves = [
        remote(half_out.at[p], half_in.at[p], half_send.at[p], half_recv.at[p], ctx_id(twin))
        for p in range(PARTS)
    ]
    store_acc = [
        pltpu.make_async_copy(acc.at[x, p], weight_grad_hbm.at[:, parts[p]], store_sem.at[3 + p])
        for p in range(PARTS)
    ]

    for p in range(PARTS):

        @pl.when(middle == 0)
        def _():
            along(order[3], 1, p).wait_recv()

        half_out[p] = ((acc[1 - x, p] + product(3, 1 - x, p)) * norm_factor).astype(bf16)
        halves[p].start()

    gather_states(states_back, -1, back_slots)
    for g in range(2):
        returning = total[g] * (second_half + first_half * decays[g] * second_whole) + back_twin[g] * first_half
        carried = stacked_left(returning)
        for r in range(4):
            rows = pl.ds(g * half_rows + r * piece, piece)
            spread = filtered_ref[rows, :] + dot(carried[r * piece : (r + 1) * piece], back_maps[g], NN)
            grads[1, rows, :] = (spread * value[rows, :].astype(f32)).astype(bf16)
            grads[2, rows, :] = (spread * key[rows, :].astype(f32)).astype(bf16)
    stores[1].start()
    stores[2].start()

    for p in range(PARTS):
        own = product(0, x, p)
        for k in range(1, 4):
            own += product(k, x, p)
        halves[p].wait_recv()
        acc[x, p] = own * norm_factor + half_in[p].astype(f32)
        store_acc[p].start()

    for origin in range(4):
        for side in (1, -1):

            @pl.when(goes(side) & (origin <= z if side > 0 else origin >= z))
            def _():
                for p in range(PARTS):
                    along(origin, side, p).wait_send()

    for copies in (states_ahead, states_back):
        for there, out, _, _, _ in copies:

            @pl.when(there)
            def _():
                out.wait_send()

    for copy in to_mate + across_copies + [to_twin_state, back_twin_state] + halves:
        copy.wait_send()
    for a in range(3):
        for there, origin, to, side, b in hops(a):

            @pl.when(there)
            def _():
                hop(origin, to, side, a, b).wait_send()

    for out, back in turns:
        out.wait_send()
    for k in range(4):
        wide(0, k, ch, across).wait_send()
        wide(1, k, ch, mate).wait_send()
        wide(2, k, across, mate).wait_send()
    for copy in stores + store_acc:
        copy.wait()


def fused(query_input, key_input, value_input, decay_rate, residue, doc_ends, out_weight, out_cotangent):
    rows, length = query_input.shape
    width = out_cotangent.shape[1]
    groups, poles = decay_rate.shape
    n_ctx, n_ch = lax.axis_size("ctx"), lax.axis_size("ch")
    piece = rows // 2 // n_ch
    anywhere = pl.BlockSpec(memory_space=pl.ANY)
    vmem = pl.BlockSpec(memory_space=pltpu.VMEM)
    smem = pl.BlockSpec(memory_space=pltpu.SMEM)
    f32, bf16 = jnp.float32, jnp.bfloat16
    dma = pltpu.SemaphoreType.DMA
    state = (groups, poles, rows // groups)
    maps = (groups, 3 * poles, length)
    block = (rows, length)
    return pl.pallas_call(
        fused_kernel,
        out_shape=tuple(jax.ShapeDtypeStruct(block, bf16) for _ in range(3))
        + (jax.ShapeDtypeStruct((rows // 2, width), f32),),
        in_specs=[smem, vmem, vmem] + [anywhere] * 5,
        out_specs=(anywhere,) * 4,
        scratch_shapes=[
            pltpu.VMEM(block, bf16), pltpu.VMEM(block, bf16), pltpu.VMEM(block, bf16),
            pltpu.VMEM((length, width), bf16),
            pltpu.VMEM((4, PARTS, length, width // PARTS), bf16),
            pltpu.VMEM((n_ch, rows, width), bf16),
            pltpu.VMEM((3,) + block, f32),
            pltpu.VMEM((2,) + block, f32),
            pltpu.VMEM(block, bf16), pltpu.VMEM(block, bf16),
            pltpu.VMEM((groups, length, length), bf16), pltpu.VMEM((groups, length, length), bf16),
            pltpu.VMEM(block, bf16), pltpu.VMEM(block, bf16),
            pltpu.VMEM(block, f32),
            pltpu.VMEM((2, n_ch, piece, length), bf16),
            pltpu.VMEM((n_ctx, piece, length), bf16),
            pltpu.VMEM((4, 4, 2, piece, length), bf16),
            pltpu.VMEM((4, n_ch, 2, piece, length), bf16),
            pltpu.VMEM((3,) + block, bf16),
            pltpu.VMEM((2, PARTS, rows // 2, width // PARTS), f32),
            pltpu.VMEM((PARTS, rows // 2, width // PARTS), bf16), pltpu.VMEM((PARTS, rows // 2, width // PARTS), bf16),
            pltpu.VMEM(state, f32), pltpu.VMEM(state, f32), pltpu.VMEM((4,) + state, f32), pltpu.VMEM(state, f32),
            pltpu.VMEM(state, f32), pltpu.VMEM(state, f32), pltpu.VMEM((4,) + state, f32), pltpu.VMEM(state, f32),
            pltpu.VMEM(state, f32),
            pltpu.VMEM(maps, bf16), pltpu.VMEM(maps, bf16),
            dma((PARTS,)), dma((4,)), dma((4,)), dma((3 + PARTS,)), dma((3,)),
            dma((2, PARTS, 4)), dma((PARTS, 4)), dma((PARTS,)), dma((PARTS,)),
            dma((2,)), dma((2,)), dma((4,)), dma((4,)),
            dma(()), dma(()), dma((4,)), dma((4,)), dma(()), dma(()), dma((4,)), dma((4,)),
            dma((8,)), dma((8,)), dma((2, 3, 4)), dma((4, 4)), dma((3, 4)), dma((3, 4)),
        ],
        compiler_params=pltpu.CompilerParams(
            collective_id=0, has_side_effects=True, vmem_limit_bytes=VMEM_LIMIT
        ),
        cost_estimate=pl.CostEstimate(flops=10_000_000_000, bytes_accessed=30_000_000, transcendentals=100_000),
        name="fused",
    )(doc_ends, decay_rate, residue, query_input, key_input, value_input, out_weight, out_cotangent)


def move_by_collectives(cotangent, weight, part, near, query, ahead, behind, in_map, out_map):
    n_ctx, n_ch = lax.axis_size("ctx"), lax.axis_size("ch")
    groups = part.shape[0]
    rows, length = query.shape
    query_f = query.astype(jnp.float32)
    cots = lax.all_gather(cotangent, "ctx", axis=0, tiled=True)
    partial_grad = lax.dot_general(
        weight, cotangent, (((1,), (1,)), ((), ())), preferred_element_type=jnp.float32
    )
    output_grad = lax.psum_scatter(partial_grad, "ch", scatter_dimension=0, tiled=True)
    entering = jnp.sum(ahead * lax.all_gather(part, "ctx", axis=0), axis=0)
    carried = jnp.einsum("gnc,gnt->gct", entering, in_map, precision=HIGH).reshape(rows, length)
    filtered = near + carried
    gathered = exchange_rows((query_f * filtered).astype(jnp.bfloat16), n_ctx, n_ch)
    signal = output_grad * query_f
    back_part = jnp.einsum("gnl,gcl->gnc", out_map, signal.reshape(groups, rows // groups, length), precision=HIGH)
    returning = jnp.sum(behind * lax.all_gather(back_part, "ctx", axis=0), axis=0)
    query_grad = (output_grad * filtered).astype(jnp.bfloat16)
    return signal, query_grad, returning, gathered, cots


def local(
    query_input, key_input, value_input, decay_rate, residue, doc_ends, out_weight, out_cotangent
):
    rows_here, length = query_input.shape
    n_ctx, n_ch = lax.axis_size("ctx"), lax.axis_size("ch")
    groups = decay_rate.shape[0]
    if (n_ctx, n_ch, groups) == (8, 4, 2) and rows_here == 1024 and length == 512:
        return fused(
            query_input, key_input, value_input, decay_rate, residue, doc_ends, out_weight, out_cotangent
        )
    group_rows = rows_here // groups
    me = lax.axis_index("ctx")
    offsets = jnp.arange(length, dtype=jnp.int32)
    place = offsets.astype(jnp.float32)
    doc_ids = doc_of(doc_ends, me * length + offsets)
    blocks = jnp.arange(n_ctx, dtype=jnp.int32)
    last_ids = doc_of(doc_ends, (blocks + 1) * length - 1)
    previous = jnp.where(me > 0, jnp.sum((doc_ends <= me * length - 1).astype(jnp.int32)), -1)
    last = doc_ids[-1]

    alive_mask = (doc_ids == previous).astype(jnp.float32)
    tail_mask = (doc_ids == last).astype(jnp.float32)
    rate = decay_rate[:, :, None]
    carry_in_map = residue[:, :, None] * jnp.exp(-rate * (place + 1.0)) * alive_mask
    carry_out_map = jnp.exp(-rate * (length - 1.0 - place)) * tail_mask
    back_out_map = jnp.exp(-rate * place) * alive_mask
    back_in_map = residue[:, :, None] * jnp.exp(-rate * (length - place)) * tail_mask
    steps_ahead = me - 1 - blocks
    joined_ahead = (steps_ahead >= 0) & (last_ids == previous)
    ahead_weight = jnp.where(
        joined_ahead[:, None, None],
        jnp.exp(-decay_rate[None] * (length * jnp.maximum(steps_ahead, 0)).astype(jnp.float32)[:, None, None]),
        0.0,
    )
    steps_back = blocks - 1 - me
    before_ids = jnp.concatenate([jnp.full((1,), -1, jnp.int32), last_ids[:-1]])
    joined_back = (steps_back >= 0) & (before_ids == last)
    back_weight = jnp.where(
        joined_back[:, None, None],
        jnp.exp(-decay_rate[None] * (length * jnp.maximum(steps_back, 0)).astype(jnp.float32)[:, None, None]),
        0.0,
    )

    key_f = key_input.astype(jnp.float32)
    value_f = value_input.astype(jnp.float32)
    mixed = (key_f * value_f).reshape(groups, group_rows, length)
    forward_part = jnp.einsum("gnl,gcl->gnc", carry_out_map, mixed, precision=HIGH)
    kernel = local_kernel(decay_rate, residue, doc_ids, length)
    near = jnp.einsum("gcs,gts->gct", mixed, kernel, precision=HIGH).reshape(rows_here, length)
    wide = (n_ctx,) + forward_part.shape
    signal, query_grad, returning, gated_rows, cotangent_all = move_by_collectives(
        out_cotangent,
        out_weight,
        forward_part,
        near,
        query_input,
        jnp.broadcast_to(ahead_weight[..., None], wide),
        jnp.broadcast_to(back_weight[..., None], wide),
        carry_in_map,
        back_out_map,
    )
    signal = signal.reshape(groups, group_rows, length)
    spread = jnp.einsum("gct,gts->gcs", signal, kernel, precision=HIGH)
    spread = spread + jnp.einsum("gnc,gns->gcs", returning, back_in_map, precision=HIGH)
    spread = spread.reshape(rows_here, length)
    key_grad = (spread * value_f).astype(jnp.bfloat16)
    value_grad = (spread * key_f).astype(jnp.bfloat16)

    norm_factor = 1.0 / math.sqrt(length * n_ctx)
    weight_grad = jnp.dot(gated_rows, cotangent_all, preferred_element_type=jnp.float32) * norm_factor
    return (query_grad, key_grad, value_grad, weight_grad)


def solution(mesh):
    return jax.shard_map(
        local,
        mesh=mesh,
        in_specs=(
            P("ch", "ctx"),
            P("ch", "ctx"),
            P("ch", "ctx"),
            P("ch", None),
            P("ch", None),
            P(),
            P(None, "ch"),
            P("ctx", "ch"),
        ),
        out_specs=(P("ch", "ctx"), P("ch", "ctx"), P("ch", "ctx"), P("ctx", "ch")),
        check_vma=False,
    )
```
